256 devices in a mesh: prow: 8 (over y, core), pcol: 32 (over x, z).
Axes of the slice: x: 4, y: 4, z: 8, core: 2. Of those that a mesh axis runs over, the one named last changes fastest.
Arguments:
- diag_one: float32 [1024, 1024], P('pcol')
- top_rows: bfloat16 [1024, 1024], P('pcol'), may hold values from -0.1875 to 0.1875
- panel_one: bfloat16 [131072, 1024], P(('prow', 'pcol')), may hold values from -6 to 6
- first_block: int32 [512], P(('prow', 'pcol')), may hold values from 0 to 3
- target: int32 [512], P(('prow', 'pcol')), may hold values from 0 to 511, as said below
- diag_two: float32 [1024, 1024], P('pcol'), may hold values from -6 to 6
- panel_two: bfloat16 [131072, 1024], P(('prow', 'pcol')), may hold values from -6 to 6
Outputs:
- panel_factor: bfloat16 [131072, 1024], P(('prow', 'pcol'))
- top_factor: bfloat16 [1024, 1024], P('pcol')
- diag_next: float32 [1024, 1024], P('pcol')
- panel_next: float32 [131072, 1024], P(('prow', 'pcol'))
The draws below stay inside these ranges and needn't reach their ends.
Inputs may be any that keep to these rules, and one draw needn't show every extreme that they name: Row block t of the second supernode is held by grid row (t // 2) // 32 and grid column (t // 2) % 32; target[i] lies in the grid column of row block i; the 2 row blocks of one device go to 2 different grid rows; in every grid column one grid row receives a row block from every grid row.
All inputs are finite; a program needn't handle non-finite values.
Results may differ from the reference program's by a relative error of at most 0.0021.
Values may be sent and summed in bfloat16 or wider, within the bound.
A program may use at most 128 MiB of HBM per device.

```python
import math
import jax
import jax.numpy as jnp
from jax import lax

W = 1024
B = 256
RB_DEV = 2
NRB = 512
N_PROW = 8
N_PCOL = 32
DEVICES = 256


def draw_diag_one(key, part):
    key_off, key_diag = jax.random.split(key, 2)
    noise = jax.random.uniform(key_off, (W, W), jnp.float32, -1.0, 1.0)
    index = jnp.arange(W)
    coupling_scale = 0.96 / math.sqrt(W)
    coupled = 0.5 * (noise + noise.T) * coupling_scale
    coupled = jnp.where(index[:, None] != index[None, :], coupled, 0.0)
    diagonal = 1.5 + jax.random.uniform(key_diag, (W,), jnp.float32)
    return (coupled + jnp.diag(diagonal)).astype(jnp.float32)


def draw_target(key, part):
    key_hot, key_order, key_turn, key_slot = jax.random.split(key, 4)
    hot_row = jax.random.randint(key_hot, (N_PCOL,), 0, N_PROW)
    device = jnp.arange(DEVICES)
    grid_col = device % N_PCOL
    hot_each = hot_row[grid_col]
    scores = jax.random.randint(key_order, (DEVICES, N_PROW - 1), 0, 1 << 20) * N_PROW + jnp.arange(N_PROW - 1)[None, :]
    order = jnp.argsort(scores, axis=1).astype(jnp.int32)
    offsets = jnp.concatenate([jnp.zeros((DEVICES, 1), jnp.int32), order + 1], axis=1)[:, :RB_DEV]
    turn = jax.random.randint(key_turn, (DEVICES,), 0, RB_DEV)
    picked = (jnp.arange(RB_DEV)[None, :] + turn[:, None]) % RB_DEV
    chosen = jnp.take_along_axis(offsets, picked, axis=1)
    dest_row = (hot_each[:, None] + chosen) % N_PROW
    slot = jax.random.randint(key_slot, (DEVICES, RB_DEV), 0, RB_DEV)
    result = (dest_row * N_PCOL + grid_col[:, None]) * RB_DEV + slot
    return result.reshape(-1).astype(jnp.int32)


def set_ends(entries, key, least, largest):
    shape = entries.shape
    place = [jax.random.randint(jax.random.fold_in(key, axis), (), 0, shape[axis]) for axis in range(len(shape))]
    entries = entries.at[tuple(place)].set(least)
    longest = shape.index(max(shape))
    place[longest] = (place[longest] + 1) % shape[longest]
    return entries.at[tuple(place)].set(largest)


def levels(stream_key, dims, cuts, least, top_value):
    gain, own = 1.0, jax.random.fold_in(stream_key, 6)
    for axis_at, parts in cuts:
        steps = jnp.exp(jax.random.uniform(jax.random.fold_in(own, axis_at), (parts,), jnp.float32, least / len(cuts), top_value / len(cuts)))
        gain = gain * jnp.repeat(steps, dims[axis_at] // parts).reshape([-1 if axis == axis_at else 1 for axis in range(len(dims))])
    return gain


def bell_draw(rng, shape, scale, limit, cuts=(), kind=jnp.bfloat16):
    factor_of = levels(rng, shape, cuts, -0.22, 0.18) if cuts else 1.0
    entries = jax.random.normal(rng, shape, jnp.float32) * scale * factor_of
    return jnp.minimum(jnp.maximum(entries, -limit), limit).astype(kind)


def setup_inputs(seed: int = 0) -> dict:
    keys = jax.random.split(jax.random.key(seed), 8)
    return {
        "diag_one": draw_diag_one(jax.random.fold_in(keys[7], 71), 0),
        "top_rows": bell_draw(keys[1], (W, W), W ** -0.5, 0.1875, ((0, 32),)),
        "panel_one": bell_draw(keys[2], (NRB * B, W), 1.0, 6.0, ((0, 256),)),
        "first_block": set_ends(jax.random.randint(keys[3], (NRB,), 0, W // B), jax.random.fold_in(keys[3], 1), 0, (W // B) - 1).astype(jnp.int32),
        "target": draw_target(jax.random.fold_in(keys[7], 71), 0),
        "diag_two": bell_draw(keys[5], (W, W), 1.0, 6.0, ((0, 32),), jnp.float32),
        "panel_two": bell_draw(keys[6], (NRB * B, W), 1.0, 6.0, ((0, 256),)),
    }


def solve_rows(factor, operand):
    return lax.linalg.triangular_solve(factor, operand, left_side=False, lower=True, transpose_a=True)

def reference(diag_one, top_rows, panel_one, first_block, target, diag_two, panel_two):
    factor = jnp.linalg.cholesky(diag_one)
    top_factor = solve_rows(factor, top_rows.astype(jnp.float32)).astype(jnp.bfloat16)
    col_count = diag_one.shape[1]
    block_count = first_block.shape[0]
    col_block = jnp.arange(col_count, dtype=jnp.int32) // B
    stacked = panel_one.reshape(block_count, B, col_count)

    def one_block(item):
        block_in, first = item
        masked = jnp.where(col_block[None, :] >= first, block_in, jnp.zeros_like(block_in))
        solved = solve_rows(factor, masked.astype(jnp.float32)).astype(jnp.bfloat16)
        update = jnp.dot(solved.astype(jnp.float32), top_factor.T.astype(jnp.float32), preferred_element_type=jnp.float32).astype(jnp.bfloat16)
        return (solved, update)
    panel_blocks, update_blocks = lax.map(one_block, (stacked, first_block))
    widened = lax.optimization_barrier(update_blocks).astype(jnp.float32)
    summed = jax.ops.segment_sum(widened, target, num_segments=panel_two.shape[0] // B)
    panel_next = panel_two.astype(jnp.float32) - summed.reshape(-1, col_count)
    diag_next = diag_two - jnp.dot(top_factor.astype(jnp.float32), top_factor.T.astype(jnp.float32), preferred_element_type=jnp.float32)
    return (panel_blocks.reshape(-1, col_count), top_factor, diag_next, panel_next)
```

```python
import functools

import jax
import jax.numpy as jnp
from jax import lax
from jax.experimental import pallas as pl
from jax.experimental.pallas import tpu as pltpu
from jax.sharding import PartitionSpec as P

F32, BF16 = jnp.float32, jnp.bfloat16
NB = 128


def split2(x):
    hi = x.astype(BF16)
    lo = (x - hi.astype(F32)).astype(BF16)
    return hi, lo


def tdot(left, right):
    return lax.dot_general(left, right, (((0,), (0,)), ((), ())), preferred_element_type=F32)


def row_bcast(x, k):
    return jnp.broadcast_to(x[k:k + 1, :], (8, x.shape[1]))


def factor_block(m_ref, t_ref, G):
    n = NB
    sub = lax.broadcasted_iota(jnp.int32, (8, n), 0)
    lane = lax.broadcasted_iota(jnp.int32, (8, n), 1)
    for s in range(n // G):
        r0 = s * G
        nch = G // 8
        raw = [m_ref[r0 + 8 * c:r0 + 8 * c + 8, :] for c in range(nch)]
        cols = {}
        for j in range(G):
            for c in range(j // 8, nch):
                cols[j, c] = jnp.broadcast_to(raw[c][:, r0 + j:r0 + j + 1], (8, n))
        inside = (lane >= r0) & (lane < r0 + G)
        band = [
            jnp.where(inside, (lane == sub + (r0 + 8 * c)).astype(F32), raw[c]) for c in range(nch)
        ]
        dvec = [None] * nch
        for k in range(G):
            kc, kr = k // 8, k % 8
            piv = row_bcast(cols[k, kc], kr)
            dvec[kc] = piv if kr == 0 else jnp.where(sub >= kr, piv, dvec[kc])
            rd = 1.0 / piv
            mult = {}
            for c in range(kc, nch):
                mult[c] = cols[k, c] * rd
            mult[kc] = jnp.where(sub > kr, mult[kc], 0.0)
            for j in range(k + 1, G):
                jc = j // 8
                other = row_bcast(cols[k, jc], j % 8)
                for c in range(jc, nch):
                    cols[j, c] = cols[j, c] - mult[c] * other
            row = row_bcast(band[kc], kr)
            for c in range(kc, nch):
                band[c] = band[c] - mult[c] * row
        band = [band[c] * lax.rsqrt(dvec[c]) for c in range(nch)]
        for c in range(nch):
            t_ref[r0 + 8 * c:r0 + 8 * c + 8, :] = jnp.where(lane < r0 + G, band[c], 0.0)
        if r0 + G < n:
            r = jnp.concatenate(band, axis=0)
            hi, lo = split2(r)
            prod = tdot(jnp.concatenate([hi, hi, lo], axis=0), jnp.concatenate([hi, lo, hi], axis=0))
            lane_all = lax.broadcasted_iota(jnp.int32, (n - r0 - G, n), 1)
            keep = (lane_all < r0) | (lane_all >= r0 + G)
            m_ref[r0 + G:, :] = jnp.where(keep, m_ref[r0 + G:, :], 0.0) - prod[r0 + G:, :]


def chol_kernel(G, a_ref, hi_ref, lo_ref, w, m, t, left, right):
    n = w.shape[0]
    steps = n // NB
    w[...] = a_ref[...]

    def step(b, carry):
        o = pl.multiple_of(b * NB, NB)
        mine = pl.ds(o, NB)
        m[...] = w[mine, mine]
        factor_block(m, t, G)
        th, tl = split2(t[...])
        wh, wl = split2(w[mine, :])
        r = jnp.dot(jnp.concatenate([th, th, tl], axis=1), jnp.concatenate([wh, wl, wh], axis=0),
                    preferred_element_type=F32)
        w[mine, :] = r
        w[mine, mine] = t[...]
        rh, rl = split2(w[mine, :])
        left[0:NB, :] = rh
        left[NB:2 * NB, :] = rh
        left[2 * NB:, :] = rl
        right[0:NB, :] = rh
        right[NB:2 * NB, :] = rl
        right[2 * NB:, :] = rh
        done = lax.broadcasted_iota(jnp.int32, (NB, n), 1) < o + NB
        hi_ref[mine, :] = jnp.where(done, rh, jnp.zeros_like(rh))
        lo_ref[mine, :] = jnp.where(done, rl, jnp.zeros_like(rl))

        def trail(i, carry):
            below = pl.ds(pl.multiple_of(i * NB, NB), NB)
            w[below, mine] = jnp.zeros((NB, NB), F32)
            w[below, :] = w[below, :] - tdot(left[:, below], right[...])
            return carry

        lax.fori_loop(b + 1, steps, trail, 0)
        return carry

    lax.fori_loop(0, steps, step, 0)


def inverse_factor(a):
    n = a.shape[0]
    whole = pl.BlockSpec(memory_space=pltpu.VMEM)
    return pl.pallas_call(
        functools.partial(chol_kernel, 32),
        out_shape=[jax.ShapeDtypeStruct((n, n), BF16)] * 2,
        in_specs=[whole],
        out_specs=[whole] * 2,
        scratch_shapes=[
            pltpu.VMEM((n, n), F32),
            pltpu.VMEM((NB, NB), F32),
            pltpu.VMEM((NB, NB), F32),
            pltpu.VMEM((3 * NB, n), BF16),
            pltpu.VMEM((3 * NB, n), BF16),
        ],
        compiler_params=pltpu.CompilerParams(vmem_limit_bytes=40 << 20),
        cost_estimate=pl.CostEstimate(flops=40 * n**3, bytes_accessed=8 * n * n, transcendentals=0),
    )(a)


def ndot(left, right):
    return lax.dot_general(left, right, (((1,), (1,)), ((), ())), preferred_element_type=F32)


def solve_into(rows, hi_ref, lo_ref, store):
    n = hi_ref.shape[0]
    for j in range(n // 256):
        cut = slice(256 * j, 256 * j + 256)
        upto = slice(0, 256 * j + 256)
        part = rows[:, upto]
        out = ndot(part, hi_ref[cut, upto]) + ndot(part, lo_ref[cut, upto])
        store(cut, out.astype(BF16))


def apply_kernel(
    tops, owns, info, hi_ref, lo_ref, top_ref, own_ref, inc_ref, two_ref, diag_ref,
    pf_ref, tf_ref, dn_ref, pn_ref, tf, solved,
):
    i = pl.program_id(0)
    rows, n = top_ref.shape

    @pl.when(i == 0)
    def _():
        pn_ref[...] = two_ref[...].astype(F32)

    @pl.when(i < tops)
    def _():
        at = pl.ds(pl.multiple_of(i * rows, rows), rows)

        def store(cut, value):
            tf[at, cut] = value

        solve_into(top_ref[...], hi_ref, lo_ref, store)

    @pl.when((i >= tops) & (i < tops + owns))
    def _():
        column = lax.broadcasted_iota(jnp.int32, (rows, n), 1)
        x = own_ref[...].astype(F32)
        x = jnp.where(column >= info[1 + i - tops] * rows, x, 0.0).astype(BF16)

        def store(cut, value):
            pf_ref[:, cut] = value

        solve_into(x, hi_ref, lo_ref, store)

    @pl.when(i == tops)
    def _():
        local = tf_ref.shape[0]
        own = tf[pl.ds(pl.multiple_of(info[0] * local, local), local), :]
        tf_ref[...] = own
        dn_ref[...] = diag_ref[...] - ndot(own, tf[...])

    @pl.when(i >= tops + owns)
    def _():
        slot = info[1 + owns + i - tops - owns]

        @pl.when(slot >= 0)
        def _():
            def store(cut, value):
                solved[:, cut] = value

            solve_into(inc_ref[0], hi_ref, lo_ref, store)
            at = pl.ds(pl.multiple_of(slot * rows, rows), rows)
            update = ndot(solved[...], tf[...]).astype(BF16).astype(F32)
            pn_ref[at, :] = pn_ref[at, :] - update


def apply(info, hi, lo, top, own, incoming, two, diag_two):
    n = hi.shape[0]
    sources, rows, _ = incoming.shape
    tops, owns = n // rows, own.shape[0] // rows
    local = diag_two.shape[0]
    fixed = lambda *shape: pl.BlockSpec(shape, lambda i, info: (0,) * len(shape))
    clip = lambda i, low, count: jnp.minimum(jnp.maximum(i - low, 0), count - 1)
    return pl.pallas_call(
        functools.partial(apply_kernel, tops, owns),
        out_shape=[
            jax.ShapeDtypeStruct(own.shape, BF16),
            jax.ShapeDtypeStruct((local, n), BF16),
            jax.ShapeDtypeStruct((local, n), F32),
            jax.ShapeDtypeStruct(two.shape, F32),
        ],
        grid_spec=pltpu.PrefetchScalarGridSpec(
            num_scalar_prefetch=1,
            grid=(tops + owns + sources,),
            in_specs=[
                fixed(n, n), fixed(n, n),
                pl.BlockSpec((rows, n), lambda i, info: (clip(i, 0, tops), 0)),
                pl.BlockSpec((rows, n), lambda i, info: (clip(i, tops, owns), 0)),
                pl.BlockSpec((1, rows, n), lambda i, info: (clip(i, tops + owns, sources), 0, 0)),
                fixed(*two.shape), fixed(local, n),
            ],
            out_specs=[
                pl.BlockSpec((rows, n), lambda i, info: (clip(i, tops, owns), 0)),
                fixed(local, n), fixed(local, n), fixed(*two.shape),
            ],
            scratch_shapes=[pltpu.VMEM((n, n), BF16), pltpu.VMEM((rows, n), BF16)],
        ),
        compiler_params=pltpu.CompilerParams(vmem_limit_bytes=48 << 20),
    )(info, hi, lo, top, own, incoming, two, diag_two)


def on_device(diag_one, top_rows, panel_one, first_block, target, diag_two, panel_two):
    n = diag_one.shape[1]
    blocks = first_block.shape[0]
    rows = panel_one.shape[0] // blocks
    grid_rows = lax.axis_size("prow")
    grid_cols = lax.axis_size("pcol")
    whole_diag = lax.all_gather(diag_one, "pcol", axis=0, tiled=True)
    whole_top = lax.all_gather(top_rows, "pcol", axis=0, tiled=True)
    dest_row = target // (blocks * grid_cols)
    dest_slot = target % blocks
    routing = dest_row[None, :] == jnp.arange(grid_rows, dtype=jnp.int32)[:, None]
    send_slot = jnp.sum(jnp.where(routing, dest_slot[None, :] + 1, 0), axis=1) - 1
    column = jnp.arange(n, dtype=jnp.int32)[None, :] // rows
    zero = jnp.zeros((), BF16)
    outgoing = jnp.zeros((grid_rows, rows, n), BF16)
    for r in range(blocks):
        piece = panel_one[r * rows:(r + 1) * rows]
        piece = jnp.where(column >= first_block[r], piece, zero)
        outgoing = jnp.where(routing[:, r][:, None, None], piece[None], outgoing)
    incoming = lax.all_to_all(outgoing, "prow", split_axis=0, concat_axis=0, tiled=True)
    incoming_slot = lax.all_to_all(send_slot, "prow", split_axis=0, concat_axis=0, tiled=True)
    info = jnp.concatenate(
        [lax.axis_index("pcol").astype(jnp.int32)[None], first_block, incoming_slot]
    )
    hi, lo = inverse_factor(whole_diag)
    panel_factor, top_own, diag_next, panel_next = apply(
        info, hi, lo, whole_top, panel_one, incoming, panel_two, diag_two
    )
    return (panel_factor, top_own, diag_next, panel_next)


def solution(mesh):
    whole = P(("prow", "pcol"), None)
    blocks = P(("prow", "pcol"))
    part = P("pcol", None)
    return jax.shard_map(
        on_device,
        mesh=mesh,
        in_specs=(part, part, whole, blocks, blocks, part, whole),
        out_specs=(whole, part, part, whole),
        check_vma=False,
    )
```

```python
import functools

import jax
import jax.numpy as jnp
from jax import lax
from jax.experimental import pallas as pl
from jax.experimental.pallas import tpu as pltpu
from jax.sharding import PartitionSpec as P

F32, BF16 = jnp.float32, jnp.bfloat16
NB = 128


def split2(x):
    hi = x.astype(BF16)
    lo = (x - hi.astype(F32)).astype(BF16)
    return hi, lo


def tdot(left, right):
    return lax.dot_general(left, right, (((0,), (0,)), ((), ())), preferred_element_type=F32)


def row_bcast(x, k):
    return jnp.broadcast_to(x[k:k + 1, :], (8, x.shape[1]))


def factor_block(m_ref, t_ref, G):
    n = NB
    sub = lax.broadcasted_iota(jnp.int32, (8, n), 0)
    lane = lax.broadcasted_iota(jnp.int32, (8, n), 1)
    for s in range(n // G):
        r0 = s * G
        nch = G // 8
        raw = [m_ref[r0 + 8 * c:r0 + 8 * c + 8, :] for c in range(nch)]
        cols = {}
        for j in range(G):
            for c in range(j // 8, nch):
                cols[j, c] = jnp.broadcast_to(raw[c][:, r0 + j:r0 + j + 1], (8, n))
        inside = (lane >= r0) & (lane < r0 + G)
        band = [
            jnp.where(inside, (lane == sub + (r0 + 8 * c)).astype(F32), raw[c]) for c in range(nch)
        ]
        dvec = [None] * nch
        for k in range(G):
            kc, kr = k // 8, k % 8
            piv = row_bcast(cols[k, kc], kr)
            dvec[kc] = piv if kr == 0 else jnp.where(sub >= kr, piv, dvec[kc])
            rd = 1.0 / piv
            mult = {}
            for c in range(kc, nch):
                mult[c] = cols[k, c] * rd
            mult[kc] = jnp.where(sub > kr, mult[kc], 0.0)
            for j in range(k + 1, G):
                jc = j // 8
                other = row_bcast(cols[k, jc], j % 8)
                for c in range(jc, nch):
                    cols[j, c] = cols[j, c] - mult[c] * other
            row = row_bcast(band[kc], kr)
            for c in range(kc, nch):
                band[c] = band[c] - mult[c] * row
        band = [band[c] * lax.rsqrt(dvec[c]) for c in range(nch)]
        for c in range(nch):
            t_ref[r0 + 8 * c:r0 + 8 * c + 8, :] = jnp.where(lane < r0 + G, band[c], 0.0)
        if r0 + G < n:
            r = jnp.concatenate(band, axis=0)
            hi, lo = split2(r)
            prod = tdot(jnp.concatenate([hi, hi, lo], axis=0), jnp.concatenate([hi, lo, hi], axis=0))
            lane_all = lax.broadcasted_iota(jnp.int32, (n - r0 - G, n), 1)
            keep = (lane_all < r0) | (lane_all >= r0 + G)
            m_ref[r0 + G:, :] = jnp.where(keep, m_ref[r0 + G:, :], 0.0) - prod[r0 + G:, :]


NX, NZ = 4, 8
MESH = pl.DeviceIdType.MESH


def eliminate(b, w, m, t, left, right, hi_ref, lo_ref):
    n = w.shape[1]
    o = pl.multiple_of(b * NB, NB)
    mine = pl.ds(o, NB)
    m[...] = w[mine, mine]
    factor_block(m, t, 32)
    th, tl = split2(t[...])
    wh, wl = split2(w[mine, :])
    r = jnp.dot(
        jnp.concatenate([th, th, tl], axis=1),
        jnp.concatenate([wh, wl, wh], axis=0),
        preferred_element_type=F32,
    )
    w[mine, :] = r
    w[mine, mine] = t[...]
    rh, rl = split2(w[mine, :])
    left[0:NB, :] = rh
    left[NB:2 * NB, :] = rh
    left[2 * NB:, :] = rl
    right[0:NB, :] = rh
    right[NB:2 * NB, :] = rl
    right[2 * NB:, :] = rh
    done = lax.broadcasted_iota(jnp.int32, (NB, n), 1) < o + NB
    hi_ref[mine, :] = jnp.where(done, rh, jnp.zeros_like(rh))
    lo_ref[mine, :] = jnp.where(done, rl, jnp.zeros_like(rl))

    def trail(i, carry):
        below = pl.ds(pl.multiple_of(i * NB, NB), NB)
        w[below, mine] = jnp.zeros((NB, NB), F32)
        w[below, :] = w[below, :] - tdot(left[:, below], right[...])
        return carry

    lax.fori_loop(b + 1, n // NB, trail, 0)


class Ring:
    def __init__(self, own, whole, sems, trim):
        self.own, self.whole, self.trim = own, whole, trim
        self.xsend, self.xrecv, self.zsend, self.zrecv, self.ssend, self.srecv = sems
        self.rows, self.n = own.shape
        self.prow, pcol = lax.axis_index("prow"), lax.axis_index("pcol")
        self.core = lax.rem(self.prow, 2)
        self.x, self.z = pcol // NZ, lax.rem(pcol, NZ)
        self.sibling = (self.prow + 1 - 2 * self.core, pcol)
        self.hops = (NZ // 2, NZ // 2 - 1)

    def at(self, x, z):
        return (self.prow, lax.rem(x + NX, NX) * NZ + lax.rem(z + NZ, NZ))

    def place(self, xs, zz):
        skip = self.n // NX * xs if self.trim else 0
        width = (self.n - skip) // 2
        row = pl.multiple_of((xs * NZ + zz) * self.rows, self.rows)
        return pl.ds(row, self.rows), pl.ds(pl.multiple_of(skip + self.core * width, 128), width)

    def xcopy(self, xs, d):
        where = self.place(xs, self.z)
        return pltpu.make_async_remote_copy(
            self.own.at[:, where[1]], self.whole.at[where], self.xsend.at[d - 1], self.xrecv.at[xs],
            device_id=self.at(xs + d, self.z), device_id_type=MESH,
        )

    def scopy(self, xs, zz, slot):
        where = self.whole.at[self.place(xs, zz)]
        return pltpu.make_async_remote_copy(
            where, where, self.ssend.at[xs, slot], self.srecv.at[xs, slot],
            device_id=self.sibling, device_id_type=MESH,
        )

    def zcopy(self, xs, zz, way, hop):
        where = self.whole.at[self.place(xs, zz)]
        return pltpu.make_async_remote_copy(
            where, where, self.zsend.at[xs, way, hop], self.zrecv.at[xs, way, hop],
            device_id=self.at(self.x, self.z + 1 - 2 * way), device_id_type=MESH,
        )

    def start(self):
        for xs in range(NX):
            @pl.when(self.x == xs)
            def _():
                for d in range(1, NX):
                    self.xcopy(xs, d).start()

    def across(self):
        for xs in range(NX):
            @pl.when(self.x != xs)
            def _():
                self.xcopy(xs, 1).wait_recv()
            for way in range(2):
                self.zcopy(xs, self.z, way, 0).start()
        for xs in range(NX):
            @pl.when(self.x != xs)
            def _():
                self.scopy(xs, self.z, 0).start()

    def hop(self, hop):
        for way in range(2):
            if hop >= self.hops[way]:
                continue
            back = self.z - hop - 1 if way == 0 else self.z + hop + 1
            back = lax.rem(back + NZ, NZ)
            for xs in range(NX):
                self.zcopy(xs, back, way, hop).wait_recv()
                if hop + 1 < self.hops[way]:
                    self.zcopy(xs, back, way, hop + 1).start()
                self.scopy(xs, back, 1 + hop + way * (NZ // 2)).start()

    def finish(self):
        for xs in range(NX):
            @pl.when(self.x != xs)
            def _():
                self.scopy(xs, self.z, 0).wait_recv()
            for slot in range(1, NZ):
                self.scopy(xs, self.z, slot).wait_recv()

    def drain(self):
        for xs in range(NX):
            @pl.when(self.x == xs)
            def _():
                for d in range(1, NX):
                    self.xcopy(xs, d).wait_send()

            @pl.when(self.x != xs)
            def _():
                self.scopy(xs, self.z, 0).wait_send()
            for way in range(2):
                for hop in range(self.hops[way]):
                    self.zcopy(xs, self.z, way, hop).wait_send()
            for slot in range(1, NZ):
                self.scopy(xs, self.z, slot).wait_send()


def factor_kernel(
    first_ref, target_ref, diag_ref, top_ref, panel_ref,
    hi_ref, lo_ref, tops_ref, inc_ref, marks_ref,
    w, m, t, left, right, panel, outgoing, mark, local, *sems,
):
    grid_rows, rows, n = inc_ref.shape
    blocks = panel.shape[0] // rows
    diag = Ring(diag_ref, w, sems[0:6], True)
    top = Ring(top_ref, tops_ref, sems[6:12], False)
    psend, precv, msend, mrecv = sems[12:]
    prow, pcol = diag.prow, lax.axis_index("pcol")
    own_rows = pl.ds(pl.multiple_of(pcol * diag.rows, diag.rows), diag.rows)

    barrier = pltpu.get_barrier_semaphore()
    peers = [diag.at(diag.x + d, diag.z) for d in range(1, NX)]
    peers += [diag.at(diag.x, diag.z + 1), diag.at(diag.x, diag.z - 1)]
    peers += [(lax.rem(prow + d, grid_rows), pcol) for d in range(1, grid_rows)]
    for peer in peers:
        pl.semaphore_signal(barrier, inc=1, device_id=peer, device_id_type=MESH)
    load = pltpu.make_async_copy(panel_ref, panel, local.at[0])
    load.start()
    keep_diag = pltpu.make_async_copy(diag_ref, w.at[own_rows], local.at[1])
    keep_diag.start()
    keep_top = pltpu.make_async_copy(top_ref, tops_ref.at[own_rows], local.at[2])
    keep_top.start()
    pl.semaphore_wait(barrier, len(peers))

    diag.start()
    lane = lax.broadcasted_iota(jnp.int32, mark.shape, 1)
    mark[...] = jnp.where(lane == 0, target_ref[0], target_ref[1])
    load.wait()
    column = lax.broadcasted_iota(jnp.int32, (rows, n), 1) // rows
    for p in range(grid_rows):
        out = jnp.zeros((rows, n), BF16)
        for r in range(blocks):
            goes = target_ref[r] // (blocks * NX * NZ) == p
            first = jnp.where(goes, first_ref[r], n)
            out = jnp.where(column >= first, panel[r * rows:(r + 1) * rows, :], out)
        outgoing[p] = out

    def pcopy(d):
        p = lax.rem(prow + d, grid_rows)
        return pltpu.make_async_remote_copy(
            outgoing.at[p], inc_ref.at[prow], psend.at[d - 1], precv.at[d - 1],
            device_id=(p, pcol), device_id_type=MESH,
        )

    def mcopy(d):
        p = lax.rem(prow + d, grid_rows)
        return pltpu.make_async_remote_copy(
            mark, marks_ref.at[prow], msend.at[d - 1], mrecv.at[d - 1],
            device_id=(p, pcol), device_id_type=MESH,
        )

    for d in range(1, grid_rows):
        mcopy(d).start()
        pcopy(d).start()
    keep_inc = pltpu.make_async_copy(outgoing.at[prow], inc_ref.at[prow], local.at[0])
    keep_inc.start()
    keep_mark = pltpu.make_async_copy(mark, marks_ref.at[prow], local.at[3])
    keep_mark.start()
    keep_diag.wait()
    keep_top.wait()
    diag.across()
    for hop in range(NZ // 2):
        diag.hop(hop)
    diag.finish()
    diag.drain()
    top.start()

    def step(b, carry):
        @pl.when(b == 1)
        def _():
            top.across()
        for hop in range(NZ // 2):
            @pl.when(b == 2 + hop)
            def _():
                top.hop(hop)
        eliminate(b, w, m, t, left, right, hi_ref, lo_ref)
        return carry

    lax.fori_loop(0, n // NB, step, 0)
    top.finish()
    keep_inc.wait()
    keep_mark.wait()
    top.drain()
    for d in range(1, grid_rows):
        mcopy(d).wait()
        pcopy(d).wait()


def factor(first_block, target, diag_one, top_rows, panel_one, grid_rows):
    n = diag_one.shape[1]
    blocks = first_block.shape[0]
    rows = panel_one.shape[0] // blocks
    smem = pl.BlockSpec(memory_space=pltpu.SMEM)
    vmem = pl.BlockSpec(memory_space=pltpu.VMEM)
    anywhere = pl.BlockSpec(memory_space=pl.ANY)
    dma = pltpu.SemaphoreType.DMA
    ring = [dma((NX - 1,)), dma((NX,))] + [dma((NX, 2, NZ // 2))] * 2 + [dma((NX, NZ))] * 2
    return pl.pallas_call(
        factor_kernel,
        out_shape=[
            jax.ShapeDtypeStruct((n, n), BF16),
            jax.ShapeDtypeStruct((n, n), BF16),
            jax.ShapeDtypeStruct((n, n), BF16),
            jax.ShapeDtypeStruct((grid_rows, rows, n), BF16),
            jax.ShapeDtypeStruct((grid_rows, 8, 128), jnp.int32),
        ],
        in_specs=[smem, smem, vmem, vmem, anywhere],
        out_specs=[vmem, vmem, vmem, anywhere, vmem],
        scratch_shapes=[
            pltpu.VMEM((n, n), F32),
            pltpu.VMEM((NB, NB), F32),
            pltpu.VMEM((NB, NB), F32),
            pltpu.VMEM((3 * NB, n), BF16),
            pltpu.VMEM((3 * NB, n), BF16),
            pltpu.VMEM(panel_one.shape, BF16),
            pltpu.VMEM((grid_rows, rows, n), BF16),
            pltpu.VMEM((8, 128), jnp.int32),
            dma((4,)),
        ] + ring + ring + [dma((grid_rows - 1,))] * 4,
        compiler_params=pltpu.CompilerParams(
            collective_id=0, has_side_effects=True, vmem_limit_bytes=32 << 20
        ),
    )(first_block, target, diag_one, top_rows, panel_one)


def ndot(left, right):
    return lax.dot_general(left, right, (((1,), (1,)), ((), ())), preferred_element_type=F32)


def solve_into(rows, hi_ref, lo_ref, store):
    n = hi_ref.shape[0]
    for j in range(n // 256):
        cut = slice(256 * j, 256 * j + 256)
        upto = slice(0, 256 * j + 256)
        part = rows[:, upto]
        out = ndot(part, hi_ref[cut, upto]) + ndot(part, lo_ref[cut, upto])
        store(cut, out.astype(BF16))


def apply_kernel(
    tops, owns, first_ref, marks, hi_ref, lo_ref, top_ref, own_ref, inc_ref, two_ref, diag_ref,
    pf_ref, tf_ref, dn_ref, pn_ref, tf, solved,
):
    i = pl.program_id(0)
    rows, n = top_ref.shape

    @pl.when(i == 0)
    def _():
        pn_ref[...] = two_ref[...].astype(F32)

    @pl.when(i < tops)
    def _():
        at = pl.ds(pl.multiple_of(i * rows, rows), rows)

        def store(cut, value):
            tf[at, cut] = value

        solve_into(top_ref[...], hi_ref, lo_ref, store)

    @pl.when((i >= tops) & (i < tops + owns))
    def _():
        column = lax.broadcasted_iota(jnp.int32, (rows, n), 1)
        x = own_ref[...].astype(F32)
        x = jnp.where(column >= first_ref[i - tops] * rows, x, 0.0).astype(BF16)

        def store(cut, value):
            pf_ref[:, cut] = value

        solve_into(x, hi_ref, lo_ref, store)

    @pl.when(i == tops)
    def _():
        local = tf_ref.shape[0]
        own = tf[pl.ds(pl.multiple_of(lax.axis_index("pcol") * local, local), local), :]
        tf_ref[...] = own
        dn_ref[...] = diag_ref[...] - ndot(own, tf[...])

    @pl.when(i >= tops + owns)
    def _():
        slot = -1
        for r in range(owns):
            to = marks[i - tops - owns, r]
            mine = to // (owns * lax.axis_size("pcol")) == lax.axis_index("prow")
            slot = jnp.where(mine, lax.rem(to, owns), slot)

        @pl.when(slot >= 0)
        def _():
            def store(cut, value):
                solved[:, cut] = value

            solve_into(inc_ref[0], hi_ref, lo_ref, store)
            at = pl.ds(pl.multiple_of(slot * rows, rows), rows)
            update = ndot(solved[...], tf[...]).astype(BF16).astype(F32)
            pn_ref[at, :] = pn_ref[at, :] - update


def apply(first_block, marks, hi, lo, top, own, incoming, two, diag_two):
    n = hi.shape[0]
    sources, rows, _ = incoming.shape
    tops, owns = n // rows, own.shape[0] // rows
    local = diag_two.shape[0]
    fixed = lambda *shape: pl.BlockSpec(shape, lambda i, first, marks: (0,) * len(shape))
    clip = lambda i, low, count: jnp.minimum(jnp.maximum(i - low, 0), count - 1)
    return pl.pallas_call(
        functools.partial(apply_kernel, tops, owns),
        out_shape=[
            jax.ShapeDtypeStruct(own.shape, BF16),
            jax.ShapeDtypeStruct((local, n), BF16),
            jax.ShapeDtypeStruct((local, n), F32),
            jax.ShapeDtypeStruct(two.shape, F32),
        ],
        grid_spec=pltpu.PrefetchScalarGridSpec(
            num_scalar_prefetch=2,
            grid=(tops + owns + sources,),
            in_specs=[
                fixed(n, n), fixed(n, n),
                pl.BlockSpec((rows, n), lambda i, first, marks: (clip(i, 0, tops), 0)),
                pl.BlockSpec((rows, n), lambda i, first, marks: (clip(i, tops, owns), 0)),
                pl.BlockSpec((1, rows, n), lambda i, first, marks: (clip(i, tops + owns, sources), 0, 0)),
                fixed(*two.shape), fixed(local, n),
            ],
            out_specs=[
                pl.BlockSpec((rows, n), lambda i, first, marks: (clip(i, tops, owns), 0)),
                fixed(local, n), fixed(local, n), fixed(*two.shape),
            ],
            scratch_shapes=[pltpu.VMEM((n, n), BF16), pltpu.VMEM((rows, n), BF16)],
        ),
        compiler_params=pltpu.CompilerParams(vmem_limit_bytes=28 << 20),
    )(first_block, marks, hi, lo, top, own, incoming, two, diag_two)


def on_device(diag_one, top_rows, panel_one, first_block, target, diag_two, panel_two):
    hi, lo, tops, incoming, marks = factor(
        first_block, target, diag_one, top_rows, panel_one, lax.axis_size("prow")
    )
    panel_factor, top_own, diag_next, panel_next = apply(
        first_block, marks[:, 0, :2], hi, lo, tops, panel_one, incoming, panel_two, diag_two
    )
    return (panel_factor, top_own, diag_next, panel_next)


def solution(mesh):
    whole = P(("prow", "pcol"), None)
    blocks = P(("prow", "pcol"))
    part = P("pcol", None)
    return jax.shard_map(
        on_device,
        mesh=mesh,
        in_specs=(part, part, whole, blocks, blocks, part, whole),
        out_specs=(whole, part, part, whole),
        check_vma=False,
    )
```

```python
import functools

import jax
import jax.numpy as jnp
from jax import lax
from jax.experimental import pallas as pl
from jax.experimental.pallas import tpu as pltpu
from jax.sharding import PartitionSpec as P

F32, BF16 = jnp.float32, jnp.bfloat16
NB = 128


def split2(x):
    hi = x.astype(BF16)
    lo = (x - hi.astype(F32)).astype(BF16)
    return hi, lo


def tdot(left, right):
    return lax.dot_general(left, right, (((0,), (0,)), ((), ())), preferred_element_type=F32)


def row_bcast(x, k):
    return jnp.broadcast_to(x[k:k + 1, :], (8, x.shape[1]))


def factor_block(m_ref, t_ref, G, p, work):
    n = NB
    sub = lax.broadcasted_iota(jnp.int32, (8, n), 0)
    lane = lax.broadcasted_iota(jnp.int32, (8, n), 1)
    groups = n // G
    nch = G // 8
    done = 0
    for s in range(groups):
        r0 = s * G
        band = [m_ref[r0 + 8 * c:r0 + 8 * c + 8, :] for c in range(nch)]
        window = {}
        dvec = [None] * nch

        def spread(j):
            for c in range(j // 8, nch):
                window[j, c] = jnp.broadcast_to(band[c][:, r0 + j:r0 + j + 1], (8, n))

        for j in range(min(p, G)):
            spread(j)
        for k in range(G):
            until = len(work) * (s * G + k + 1) // n
            while done < until:
                work[done]()
                done += 1
            kc, kr = k // 8, k % 8
            piv = row_bcast(window[k, kc], kr)
            dvec[kc] = piv if kr == 0 else jnp.where(sub >= kr, piv, dvec[kc])
            rd = 1.0 / piv
            mult = {c: window[k, c] * rd for c in range(kc, nch)}
            mult[kc] = jnp.where(sub > kr, mult[kc], 0.0)
            for j in range(k + 1, min(k + p, G)):
                jc = j // 8
                other = row_bcast(window[k, jc], j % 8)
                for c in range(jc, nch):
                    window[j, c] = window[j, c] - mult[c] * other
            here = lane == r0 + k
            row = jnp.where(here, 1.0, row_bcast(band[kc], kr))
            for c in range(kc, nch):
                if c == kc:
                    old = jnp.where(here & (sub >= kr), (sub == kr).astype(F32), band[c])
                else:
                    old = jnp.where(here, 0.0, band[c])
                band[c] = old - mult[c] * row
            if k + p < G:
                spread(k + p)
            for c in range(kc, nch):
                del window[k, c]
        for c in range(nch):
            band[c] = band[c] * lax.rsqrt(dvec[c])
            upper = lane > sub + (r0 + 8 * c)
            t_ref[r0 + 8 * c:r0 + 8 * c + 8, :] = jnp.where(upper, 0.0, band[c])
            band[c] = jnp.where(upper & (lane < r0 + G), 0.0, band[c])
        if r0 + G < n:
            r = jnp.concatenate(band, axis=0)
            hi, lo = split2(r)
            prod = tdot(jnp.concatenate([hi, hi, lo], axis=0), jnp.concatenate([hi, lo, hi], axis=0))
            lane_all = lax.broadcasted_iota(jnp.int32, (n - r0 - G, n), 1)
            keep = (lane_all < r0) | (lane_all >= r0 + G)
            m_ref[r0 + G:, :] = jnp.where(keep, m_ref[r0 + G:, :], 0.0) - prod[r0 + G:, :]
    while done < len(work):
        work[done]()
        done += 1


def blk(i, j=None):
    return slice(NB * i, NB * (i + 1 if j is None else j))


def eliminate(w, m, t, left, right, hi_ref, lo_ref, G, p, before, extra):
    n = w.shape[1]
    steps = n // NB

    def update(b, i, start, stop):
        prod = tdot(left[b % 2, :, blk(i)], right[b % 2, :, blk(start, stop)])
        if start == stop - 1 == b:
            w[blk(i), blk(b)] = -prod
        else:
            w[blk(i), blk(start, stop)] = w[blk(i), blk(start, stop)] - prod

    for b in range(steps):
        before(b)
        if b > 0:
            update(b - 1, b, b, b + 1)
        m[...] = w[blk(b), blk(b)]
        work = []
        if b > 0:
            for i in range(b, steps):
                if b > 1:
                    work.append(functools.partial(update, b - 1, i, 0, b - 1))
                work.append(functools.partial(update, b - 1, i, b - 1, b))
                first = max(i, b + 1)
                if first < steps:
                    work.append(functools.partial(update, b - 1, i, first, steps))
        work += extra(b)
        factor_block(m, t, G, p, work)
        th, tl = split2(t[...])
        tt = jnp.concatenate([th, th, tl], axis=1)
        slot = b % 2
        for start, stop in ((0, b), (b, b + 1), (b + 1, steps)):
            if start == stop:
                continue
            cut = blk(start, stop)
            if start == b:
                rh, rl = th, tl
            else:
                wh, wl = split2(w[blk(b), cut])
                r = jnp.dot(tt, jnp.concatenate([wh, wl, wh], axis=0), preferred_element_type=F32)
                rh, rl = split2(r)
            if start > b:
                left[slot, 0:NB, cut] = rh
                left[slot, NB:2 * NB, cut] = rh
                left[slot, 2 * NB:, cut] = rl
            else:
                hi_ref[blk(b), cut] = rh
                lo_ref[blk(b), cut] = rl
            right[slot, 0:NB, cut] = rh
            right[slot, NB:2 * NB, cut] = rl
            right[slot, 2 * NB:, cut] = rh
        if b + 1 < steps:
            hi_ref[blk(b), blk(b + 1, steps)] = jnp.zeros((NB, n - NB * (b + 1)), BF16)
            lo_ref[blk(b), blk(b + 1, steps)] = jnp.zeros((NB, n - NB * (b + 1)), BF16)


NX, NZ = 4, 8
MESH = pl.DeviceIdType.MESH


def ndot(left, right):
    return lax.dot_general(left, right, (((1,), (1,)), ((), ())), preferred_element_type=F32)


def solve_part(rows, hi_ref, lo_ref, j):
    cut, upto = slice(256 * j, 256 * j + 256), slice(0, 256 * j + 256)
    return (ndot(rows[:, upto], hi_ref[cut, upto]) + ndot(rows[:, upto], lo_ref[cut, upto])).astype(BF16)


class Ring:
    def __init__(self, own, whole, sems, trim):
        self.own, self.whole, self.trim = own, whole, trim
        self.xsend, self.xrecv, self.zsend, self.zrecv, self.ssend, self.srecv = sems
        self.rows, self.n = own.shape
        self.prow, pcol = lax.axis_index("prow"), lax.axis_index("pcol")
        self.core = lax.rem(self.prow, 2)
        self.x, self.z = pcol // NZ, lax.rem(pcol, NZ)
        self.sibling = (self.prow + 1 - 2 * self.core, pcol)
        self.hops = (NZ // 2, NZ // 2 - 1)

    def at(self, x, z):
        return (self.prow, lax.rem(x + NX, NX) * NZ + lax.rem(z + NZ, NZ))

    def place(self, xs, zz):
        skip = self.n // NX * xs if self.trim else 0
        width = (self.n - skip) // 2
        row = pl.multiple_of((xs * NZ + zz) * self.rows, self.rows)
        return pl.ds(row, self.rows), pl.ds(pl.multiple_of(skip + self.core * width, 128), width)

    def xcopy(self, xs, d):
        where = self.place(xs, self.z)
        return pltpu.make_async_remote_copy(
            self.own.at[:, where[1]], self.whole.at[where], self.xsend.at[d - 1], self.xrecv.at[xs],
            device_id=self.at(xs + d, self.z), device_id_type=MESH,
        )

    def scopy(self, xs, zz, slot):
        where = self.whole.at[self.place(xs, zz)]
        return pltpu.make_async_remote_copy(
            where, where, self.ssend.at[xs, slot], self.srecv.at[xs, slot],
            device_id=self.sibling, device_id_type=MESH,
        )

    def zcopy(self, xs, zz, way, hop):
        where = self.whole.at[self.place(xs, zz)]
        return pltpu.make_async_remote_copy(
            where, where, self.zsend.at[xs, way, hop], self.zrecv.at[xs, way, hop],
            device_id=self.at(self.x, self.z + 1 - 2 * way), device_id_type=MESH,
        )

    def start(self):
        for xs in range(NX):
            @pl.when(self.x == xs)
            def _():
                for d in range(1, NX):
                    self.xcopy(xs, d).start()

    def across(self):
        for xs in range(NX):
            @pl.when(self.x != xs)
            def _():
                self.xcopy(xs, 1).wait_recv()
            for way in range(2):
                self.zcopy(xs, self.z, way, 0).start()
        for xs in range(NX):
            @pl.when(self.x != xs)
            def _():
                self.scopy(xs, self.z, 0).start()

    def hop(self, hop):
        for way in range(2):
            if hop >= self.hops[way]:
                continue
            back = self.z - hop - 1 if way == 0 else self.z + hop + 1
            back = lax.rem(back + NZ, NZ)
            for xs in range(NX):
                self.zcopy(xs, back, way, hop).wait_recv()
                if hop + 1 < self.hops[way]:
                    self.zcopy(xs, back, way, hop + 1).start()
                self.scopy(xs, back, 1 + hop + way * (NZ // 2)).start()

    def finish(self):
        for xs in range(NX):
            @pl.when(self.x != xs)
            def _():
                self.scopy(xs, self.z, 0).wait_recv()
            for slot in range(1, NZ):
                self.scopy(xs, self.z, slot).wait_recv()

    def drain(self):
        for xs in range(NX):
            @pl.when(self.x == xs)
            def _():
                for d in range(1, NX):
                    self.xcopy(xs, d).wait_send()

            @pl.when(self.x != xs)
            def _():
                self.scopy(xs, self.z, 0).wait_send()
            for way in range(2):
                for hop in range(self.hops[way]):
                    self.zcopy(xs, self.z, way, hop).wait_send()
            for slot in range(1, NZ):
                self.scopy(xs, self.z, slot).wait_send()


class Panels:
    def __init__(self, own, whole, sems):
        self.own, self.whole = own, whole
        self.ysend, self.yrecv, self.fsend, self.frecv, self.ssend, self.srecv = sems
        self.prow, self.pcol = lax.axis_index("prow"), lax.axis_index("pcol")
        self.grid_rows = lax.axis_size("prow")
        self.core = lax.rem(self.prow, 2)

    def row(self, d):
        return lax.rem(self.prow + 2 * d + self.grid_rows, self.grid_rows)

    def copy(self, source, target, send, recv, row):
        return pltpu.make_async_remote_copy(
            source, target, send, recv, device_id=(row, self.pcol), device_id_type=MESH
        )

    def near(self, way, r):
        return self.copy(
            self.own.at[r], self.whole.at[self.prow, r], self.ysend.at[way, r], self.yrecv.at[way, r],
            self.row(1 - 2 * way),
        )

    def far(self, way):
        where = self.whole.at[self.row(2 * way - 1), way]
        return self.copy(where, where, self.fsend.at[way], self.frecv.at[way], self.row(1 - 2 * way))

    def across(self, d, r):
        where = self.whole.at[self.row(d), r]
        source = self.own.at[r] if d == 0 else where
        return self.copy(source, where, self.ssend.at[d, r], self.srecv.at[d, r], self.prow + 1 - 2 * self.core)

    def start(self):
        for r in range(2):
            for way in range(2):
                self.near(way, (r + way) % 2).start()
        for r in range(2):
            self.across(0, r).start()

    def forward(self):
        for way in range(2):
            self.near(way, way).wait_recv()
            self.far(way).start()
            self.across(3 - 2 * way, way).start()

    def pass_on(self):
        for way in range(2):
            self.near(way, 1 - way).wait_recv()
            self.across(3 - 2 * way, 1 - way).start()

    def finish(self):
        for way in range(2):
            self.far(way).wait_recv()
            self.across(2, way).start()
        for d in range(4):
            for r in range(2):
                self.across(d, r).wait()
        for way in range(2):
            self.far(way).wait_send()
            for r in range(2):
                self.near(way, r).wait_send()


def factor_kernel(
    first_ref, target_ref, diag_ref, top_ref, panel_ref,
    hi_ref, lo_ref, tf_ref, pf_ref, inc_ref, marks_ref,
    w, m, t, left, right, tops, masked, mark, local, *sems,
):
    grid_rows, blocks, rows, n = inc_ref.shape
    diag = Ring(diag_ref, w, sems[0:6], True)
    top = Ring(top_ref, tops, sems[6:12], False)
    panels = Panels(panel_ref, inc_ref, sems[12:18])
    msend, mrecv = sems[18:]
    prow, pcol = diag.prow, lax.axis_index("pcol")
    own_rows = pl.ds(pl.multiple_of(pcol * diag.rows, diag.rows), diag.rows)

    barrier = pltpu.get_barrier_semaphore()
    peers = [diag.at(diag.x + d, diag.z) for d in range(1, NX)]
    peers += [diag.at(diag.x, diag.z + 1), diag.at(diag.x, diag.z - 1)]
    peers += [(lax.rem(prow + d, grid_rows), pcol) for d in range(1, grid_rows)]
    for peer in peers:
        pl.semaphore_signal(barrier, inc=1, device_id=peer, device_id_type=MESH)
    keep_diag = pltpu.make_async_copy(diag_ref, w.at[own_rows], local.at[0])
    keep_diag.start()
    keep_top = pltpu.make_async_copy(top_ref, tops.at[own_rows], local.at[1])
    keep_top.start()
    keep_panel = pltpu.make_async_copy(panel_ref, inc_ref.at[prow], local.at[2])
    keep_panel.start()
    lane = lax.broadcasted_iota(jnp.int32, mark.shape, 1)
    word = jnp.where(lane == 0, target_ref[0], target_ref[1])
    for r in range(blocks):
        word = jnp.where(lane == blocks + r, first_ref[r], word)
    mark[...] = word
    pl.semaphore_wait(barrier, len(peers))

    diag.start()

    def mcopy(d):
        return pltpu.make_async_remote_copy(
            mark, marks_ref.at[prow], msend.at[d - 1], mrecv.at[d - 1],
            device_id=(lax.rem(prow + d, grid_rows), pcol), device_id_type=MESH,
        )

    for d in range(1, grid_rows):
        mcopy(d).start()
    keep_mark = pltpu.make_async_copy(mark, marks_ref.at[prow], local.at[3])
    keep_mark.start()
    panels.start()
    keep_diag.wait()
    keep_top.wait()
    keep_panel.wait()
    diag.across()
    for hop in range(NZ // 2):
        diag.hop(hop)
    diag.finish()
    diag.drain()
    top.start()
    column = lax.broadcasted_iota(jnp.int32, (rows, n), 1)
    for r in range(blocks):
        x = inc_ref[prow, r].astype(F32)
        masked[r * rows:(r + 1) * rows, :] = jnp.where(column >= first_ref[r] * rows, x, 0.0).astype(BF16)

    def before(b):
        if b == 1:
            top.across()
        if 2 <= b < 2 + NZ // 2:
            top.hop(b - 2)
        if b == 3:
            panels.forward()
        if b == 5:
            panels.pass_on()
        if b == 6:
            top.finish()

    def solve(x, out, j, piece):
        at = slice(512 * piece, 512 * piece + 512)
        out[at, 256 * j:256 * j + 256] = solve_part(x[at, :], hi_ref, lo_ref, j)

    def extra(b):
        own = {3: [0], 5: [1], 7: [2]}.get(b, [])
        tall = {6: [0, 1], 7: [2]}.get(b, [])
        work = [functools.partial(solve, masked, pf_ref, j, 0) for j in own]
        return work + [functools.partial(solve, tops, tf_ref, j, piece) for j in tall for piece in range(n // 512)]

    eliminate(w, m, t, left, right, hi_ref, lo_ref, 32, 12, before, extra)
    solve(masked, pf_ref, 3, 0)
    for piece in range(n // 512):
        solve(tops, tf_ref, 3, piece)
    panels.finish()
    keep_mark.wait()
    top.drain()
    for d in range(1, grid_rows):
        mcopy(d).wait()


def factor(first_block, target, diag_one, top_rows, panel_one, grid_rows):
    n = diag_one.shape[1]
    blocks = first_block.shape[0]
    rows = panel_one.shape[0] // blocks
    smem = pl.BlockSpec(memory_space=pltpu.SMEM)
    vmem = pl.BlockSpec(memory_space=pltpu.VMEM)
    hbm = pl.BlockSpec(memory_space=pltpu.HBM)
    dma = pltpu.SemaphoreType.DMA
    ring = [dma((NX - 1,)), dma((NX,))] + [dma((NX, 2, NZ // 2))] * 2 + [dma((NX, NZ))] * 2
    here = lambda v: pltpu.with_memory_space_constraint(v, pltpu.HBM)
    return pl.pallas_call(
        factor_kernel,
        out_shape=[
            jax.ShapeDtypeStruct((n, n), BF16),
            jax.ShapeDtypeStruct((n, n), BF16),
            jax.ShapeDtypeStruct((n, n), BF16),
            jax.ShapeDtypeStruct(panel_one.shape, BF16),
            jax.ShapeDtypeStruct((grid_rows, blocks, rows, n), BF16),
            jax.ShapeDtypeStruct((grid_rows, 8, 128), jnp.int32),
        ],
        in_specs=[smem, smem, hbm, hbm, hbm],
        out_specs=[vmem] * 6,
        scratch_shapes=[
            pltpu.VMEM((n, n), F32),
            pltpu.VMEM((NB, NB), F32),
            pltpu.VMEM((NB, NB), F32),
            pltpu.VMEM((2, 3 * NB, n), BF16),
            pltpu.VMEM((2, 3 * NB, n), BF16),
            pltpu.VMEM((n, n), BF16),
            pltpu.VMEM(panel_one.shape, BF16),
            pltpu.VMEM((8, 128), jnp.int32),
            dma((4,)),
        ] + ring + ring
        + [dma((2, 2))] * 2 + [dma((2,))] * 2 + [dma((4, 2))] * 2 + [dma((grid_rows - 1,))] * 2,
        compiler_params=pltpu.CompilerParams(
            collective_id=0, has_side_effects=True, vmem_limit_bytes=24 << 20
        ),
    )(first_block, target, here(diag_one), here(top_rows), here(panel_one.reshape(blocks, rows, n)))


QUAD = 4


def apply_kernel(
    marks, hi_ref, lo_ref, tf_ref, pf_ref, inc_ref, two_ref, diag_ref,
    pf_out, tf_out, dn_out, pn_out, two, diag, acc, x, solved, sems,
):
    sources, blocks, rows, n = inc_ref.shape
    local = diag.shape[0]
    prow, pcol = lax.axis_index("prow"), lax.axis_index("pcol")
    own = pl.ds(pl.multiple_of(pcol * local, local), local)
    load_two = pltpu.make_async_copy(two_ref, two, sems.at[0])
    load_two.start()
    load_diag = pltpu.make_async_copy(diag_ref, diag, sems.at[1])
    load_diag.start()
    save_pf = pltpu.make_async_copy(pf_ref, pf_out, sems.at[2])
    save_pf.start()
    save_tf = pltpu.make_async_copy(tf_ref.at[own], tf_out, sems.at[3])
    save_tf.start()
    load_diag.wait()
    diag[...] = diag[...] - ndot(tf_ref[own, :], tf_ref[...])
    save_dn = pltpu.make_async_copy(diag, dn_out, sems.at[4])
    save_dn.start()
    load_two.wait()
    acc[...] = two[...].astype(F32)
    column = lax.broadcasted_iota(jnp.int32, (rows, n), 1)

    def quad(q, carry):
        slots, some = [], []
        for i in range(QUAD):
            p = q * QUAD + i
            slot, which, here = 0, 0, False
            for r in range(blocks):
                to = marks[p, 0, r]
                mine = to // (blocks * lax.axis_size("pcol")) == prow
                slot = jnp.where(mine, lax.rem(to, blocks), slot)
                which = jnp.where(mine, r, which)
                here = mine | here
            slots.append(slot)
            some.append(here)
            first = jnp.where(here, marks[p, 0, blocks + which] * rows, n)
            x[i * rows:(i + 1) * rows, :] = jnp.where(
                column >= first, inc_ref[p, which].astype(F32), 0.0
            ).astype(BF16)
        anyone = some[0]
        for here in some[1:]:
            anyone = anyone | here

        @pl.when(anyone)
        def _():
            for j in range(n // 256):
                solved[:, 256 * j:256 * j + 256] = solve_part(x, hi_ref, lo_ref, j)
            for j in range(n // 256):
                cut = slice(256 * j, 256 * j + 256)
                update = ndot(solved[...], tf_ref[cut, :]).astype(BF16).astype(F32)
                for i in range(QUAD):
                    at = pl.ds(pl.multiple_of(slots[i] * rows, rows), rows)
                    acc[at, cut] = acc[at, cut] - update[i * rows:(i + 1) * rows, :]

        return carry

    lax.fori_loop(0, sources // QUAD, quad, 0)
    save_pn = pltpu.make_async_copy(acc, pn_out, sems.at[5])
    save_pn.start()
    for save in (save_pf, save_tf, save_dn, save_pn):
        save.wait()


def apply(marks, hi, lo, tf, pf, incoming, two, diag_two):
    n = hi.shape[0]
    rows = incoming.shape[2]
    local = diag_two.shape[0]
    smem = pl.BlockSpec(memory_space=pltpu.SMEM)
    vmem = pl.BlockSpec(memory_space=pltpu.VMEM)
    hbm = pl.BlockSpec(memory_space=pltpu.HBM)
    here = lambda v: pltpu.with_memory_space_constraint(v, pltpu.HBM)
    return pl.pallas_call(
        apply_kernel,
        out_shape=[
            jax.ShapeDtypeStruct(pf.shape, BF16),
            jax.ShapeDtypeStruct((local, n), BF16),
            jax.ShapeDtypeStruct((local, n), F32),
            jax.ShapeDtypeStruct(two.shape, F32),
        ],
        in_specs=[smem, vmem, vmem, vmem, vmem, vmem, hbm, hbm],
        out_specs=[hbm] * 4,
        scratch_shapes=[
            pltpu.VMEM(two.shape, BF16),
            pltpu.VMEM((local, n), F32),
            pltpu.VMEM(two.shape, F32),
            pltpu.VMEM((QUAD * rows, n), BF16),
            pltpu.VMEM((QUAD * rows, n), BF16),
            pltpu.SemaphoreType.DMA((6,)),
        ],
        compiler_params=pltpu.CompilerParams(vmem_limit_bytes=20 << 20),
    )(marks, hi, lo, tf, pf, incoming, here(two), here(diag_two))


def on_device(diag_one, top_rows, panel_one, first_block, target, diag_two, panel_two):
    hi, lo, tf, pf, incoming, marks = factor(
        first_block, target, diag_one, top_rows, panel_one, lax.axis_size("prow")
    )
    return tuple(apply(marks, hi, lo, tf, pf, incoming, panel_two, diag_two))


def solution(mesh):
    whole = P(("prow", "pcol"), None)
    blocks = P(("prow", "pcol"))
    part = P("pcol", None)
    return jax.shard_map(
        on_device,
        mesh=mesh,
        in_specs=(part, part, whole, blocks, blocks, part, whole),
        out_specs=(whole, part, part, whole),
        check_vma=False,
    )
```

```python
import functools

import jax
import jax.numpy as jnp
from jax import lax
from jax.experimental import pallas as pl
from jax.experimental.pallas import tpu as pltpu
from jax.sharding import PartitionSpec as P

F32, BF16 = jnp.float32, jnp.bfloat16
NB = 128


def split2(x):
    hi = x.astype(BF16)
    lo = (x - hi.astype(F32)).astype(BF16)
    return hi, lo


def tdot(left, right):
    return lax.dot_general(left, right, (((0,), (0,)), ((), ())), preferred_element_type=F32)


def row_bcast(x, k):
    return jnp.broadcast_to(x[k:k + 1, :], (8, x.shape[1]))


def factor_block(m_ref, t_ref, G, p, work, tick):
    n = NB
    sub = lax.broadcasted_iota(jnp.int32, (8, n), 0)
    lane = lax.broadcasted_iota(jnp.int32, (8, n), 1)
    groups = n // G
    nch = G // 8
    done = 0
    for s in range(groups):
        r0 = s * G
        tick(s)
        band = [m_ref[r0 + 8 * c:r0 + 8 * c + 8, :] for c in range(nch)]
        window = {}
        dvec = [None] * nch

        def spread(j):
            for c in range(j // 8, nch):
                window[j, c] = jnp.broadcast_to(band[c][:, r0 + j:r0 + j + 1], (8, n))

        for j in range(min(p, G)):
            spread(j)
        for k in range(G):
            until = len(work) * (s * G + k + 1) // n
            while done < until:
                work[done]()
                done += 1
            kc, kr = k // 8, k % 8
            piv = row_bcast(window[k, kc], kr)
            dvec[kc] = piv if kr == 0 else jnp.where(sub >= kr, piv, dvec[kc])
            rd = 1.0 / piv
            mult = {c: window[k, c] * rd for c in range(kc, nch)}
            mult[kc] = jnp.where(sub > kr, mult[kc], 0.0)
            for j in range(k + 1, min(k + p, G)):
                jc = j // 8
                other = row_bcast(window[k, jc], j % 8)
                for c in range(jc, nch):
                    window[j, c] = window[j, c] - mult[c] * other
            here = lane == r0 + k
            row = jnp.where(here, 1.0, row_bcast(band[kc], kr))
            for c in range(kc, nch):
                if c == kc:
                    old = jnp.where(here & (sub >= kr), (sub == kr).astype(F32), band[c])
                else:
                    old = jnp.where(here, 0.0, band[c])
                band[c] = old - mult[c] * row
            if k + p < G:
                spread(k + p)
            for c in range(kc, nch):
                del window[k, c]
        for c in range(nch):
            band[c] = band[c] * lax.rsqrt(dvec[c])
            upper = lane > sub + (r0 + 8 * c)
            t_ref[r0 + 8 * c:r0 + 8 * c + 8, :] = jnp.where(upper, 0.0, band[c])
            band[c] = jnp.where(upper & (lane < r0 + G), 0.0, band[c])
        if r0 + G < n:
            r = jnp.concatenate(band, axis=0)
            hi, lo = split2(r)
            prod = tdot(jnp.concatenate([hi, hi, lo], axis=0), jnp.concatenate([hi, lo, hi], axis=0))
            lane_all = lax.broadcasted_iota(jnp.int32, (n - r0 - G, n), 1)
            keep = (lane_all < r0) | (lane_all >= r0 + G)
            m_ref[r0 + G:, :] = jnp.where(keep, m_ref[r0 + G:, :], 0.0) - prod[r0 + G:, :]
    while done < len(work):
        work[done]()
        done += 1


def blk(i, j=None):
    return slice(NB * i, NB * (i + 1 if j is None else j))


def eliminate(w, m, t, left, right, hi_ref, lo_ref, G, p, before, tick, extra):
    n = w.shape[1]
    steps = n // NB
    slots = left.shape[0] // (3 * NB)

    def update(i, k0, k1, start, stop, fresh):
        at = 3 * NB * (k0 % slots)
        span = slice(at, at + 3 * NB * (k1 - k0))
        prod = tdot(left[span, blk(i)], right[span, blk(start, stop)])
        if fresh:
            w[blk(i), blk(start, stop)] = -prod
        else:
            w[blk(i), blk(start, stop)] = w[blk(i), blk(start, stop)] - prod

    for b in range(steps):
        before(b)
        if b > 0:
            update(b, b - 1, b, b, b + 1, False)
        m[...] = w[blk(b), blk(b)]
        work = []
        for i in range(b, steps):
            if b == 0:
                continue
            k0 = b - 1
            if k0 > 0:
                work.append(functools.partial(update, i, k0, b, 0, k0, False))
            for c in range(k0, b):
                work.append(functools.partial(update, i, c, b, c, c + 1, True))
            first = max(i, b + 1)
            if first < steps:
                work.append(functools.partial(update, i, k0, b, first, steps, False))
        work += extra(b)
        factor_block(m, t, G, p, work, functools.partial(tick, b))
        th, tl = split2(t[...])
        tt = jnp.concatenate([th, th, tl], axis=1)
        at = 3 * NB * (b % slots)
        one, two, three = (slice(at + NB * q, at + NB * q + NB) for q in range(3))
        for start, stop in ((0, b), (b, b + 1), (b + 1, steps)):
            if start == stop:
                continue
            cut = blk(start, stop)
            if start == b:
                rh, rl = th, tl
            else:
                wh, wl = split2(w[blk(b), cut])
                r = jnp.dot(tt, jnp.concatenate([wh, wl, wh], axis=0), preferred_element_type=F32)
                rh, rl = split2(r)
            if start > b:
                left[one, cut] = rh
                left[two, cut] = rh
                left[three, cut] = rl
            else:
                hi_ref[blk(b), cut] = rh
                lo_ref[blk(b), cut] = rl
            right[one, cut] = rh
            right[two, cut] = rl
            right[three, cut] = rh
        if b + 1 < steps:
            hi_ref[blk(b), blk(b + 1, steps)] = jnp.zeros((NB, n - NB * (b + 1)), BF16)
            lo_ref[blk(b), blk(b + 1, steps)] = jnp.zeros((NB, n - NB * (b + 1)), BF16)


NX, NZ = 4, 8
MESH = pl.DeviceIdType.MESH


def ndot(left, right):
    return lax.dot_general(left, right, (((1,), (1,)), ((), ())), preferred_element_type=F32)


def solve_part(rows, hi_ref, lo_ref, j):
    cut, upto = slice(256 * j, 256 * j + 256), slice(0, 256 * j + 256)
    return (ndot(rows[:, upto], hi_ref[cut, upto]) + ndot(rows[:, upto], lo_ref[cut, upto])).astype(BF16)


class Ring:
    def __init__(self, own, whole, sems, trim):
        self.own, self.whole, self.trim = own, whole, trim
        self.xsend, self.xrecv, self.zsend, self.zrecv, self.ssend, self.srecv = sems
        self.rows, self.n = own.shape
        self.prow, pcol = lax.axis_index("prow"), lax.axis_index("pcol")
        self.core = lax.rem(self.prow, 2)
        self.x, self.z = pcol // NZ, lax.rem(pcol, NZ)
        self.sibling = (self.prow + 1 - 2 * self.core, pcol)
        self.hops = (NZ // 2, NZ // 2 - 1)

    def at(self, x, z):
        return (self.prow, lax.rem(x + NX, NX) * NZ + lax.rem(z + NZ, NZ))

    def place(self, xs, zz):
        skip = self.n // NX * xs if self.trim else 0
        width = (self.n - skip) // 2
        row = pl.multiple_of((xs * NZ + zz) * self.rows, self.rows)
        return pl.ds(row, self.rows), pl.ds(pl.multiple_of(skip + self.core * width, 128), width)

    def xcopy(self, xs, d):
        where = self.place(xs, self.z)
        return pltpu.make_async_remote_copy(
            self.own.at[:, where[1]], self.whole.at[where], self.xsend.at[d - 1], self.xrecv.at[xs],
            device_id=self.at(xs + d, self.z), device_id_type=MESH,
        )

    def scopy(self, xs, zz, slot):
        where = self.whole.at[self.place(xs, zz)]
        return pltpu.make_async_remote_copy(
            where, where, self.ssend.at[xs, slot], self.srecv.at[xs, slot],
            device_id=self.sibling, device_id_type=MESH,
        )

    def zcopy(self, xs, zz, way, hop):
        where = self.whole.at[self.place(xs, zz)]
        return pltpu.make_async_remote_copy(
            where, where, self.zsend.at[xs, way, hop], self.zrecv.at[xs, way, hop],
            device_id=self.at(self.x, self.z + 1 - 2 * way), device_id_type=MESH,
        )

    def start(self):
        for xs in range(NX):
            @pl.when(self.x == xs)
            def _():
                for d in range(1, NX):
                    self.xcopy(xs, d).start()

    def across(self, groups):
        for xs in groups:
            @pl.when(self.x != xs)
            def _():
                self.xcopy(xs, 1).wait_recv()
            for way in range(2):
                self.zcopy(xs, self.z, way, 0).start()
        for xs in groups:
            @pl.when(self.x != xs)
            def _():
                self.scopy(xs, self.z, 0).start()

    def hop(self, hop, groups):
        for xs in groups:
            for way in range(2):
                if hop >= self.hops[way]:
                    continue
                back = self.z - hop - 1 if way == 0 else self.z + hop + 1
                back = lax.rem(back + NZ, NZ)
                self.zcopy(xs, back, way, hop).wait_recv()
                if hop + 1 < self.hops[way]:
                    self.zcopy(xs, back, way, hop + 1).start()
                self.scopy(xs, back, 1 + hop + way * (NZ // 2)).start()

    def finish(self, groups):
        for xs in groups:
            @pl.when(self.x != xs)
            def _():
                self.scopy(xs, self.z, 0).wait_recv()
            for slot in range(1, NZ):
                self.scopy(xs, self.z, slot).wait_recv()

    def drain(self, groups):
        for xs in groups:
            @pl.when(self.x == xs)
            def _():
                for d in range(1, NX):
                    self.xcopy(xs, d).wait_send()

            @pl.when(self.x != xs)
            def _():
                self.scopy(xs, self.z, 0).wait_send()
            for way in range(2):
                for hop in range(self.hops[way]):
                    self.zcopy(xs, self.z, way, hop).wait_send()
            for slot in range(1, NZ):
                self.scopy(xs, self.z, slot).wait_send()


class Panels:
    def __init__(self, own, whole, sems):
        self.own, self.whole = own, whole
        self.ysend, self.yrecv, self.fsend, self.frecv, self.ssend, self.srecv = sems
        self.prow, self.pcol = lax.axis_index("prow"), lax.axis_index("pcol")
        self.grid_rows = lax.axis_size("prow")
        self.core = lax.rem(self.prow, 2)

    def row(self, d):
        return lax.rem(self.prow + 2 * d + self.grid_rows, self.grid_rows)

    def copy(self, source, target, send, recv, row):
        return pltpu.make_async_remote_copy(
            source, target, send, recv, device_id=(row, self.pcol), device_id_type=MESH
        )

    def near(self, way, r):
        return self.copy(
            self.own.at[r], self.whole.at[self.prow, r], self.ysend.at[way, r], self.yrecv.at[way, r],
            self.row(1 - 2 * way),
        )

    def far(self, way):
        where = self.whole.at[self.row(2 * way - 1), way]
        return self.copy(where, where, self.fsend.at[way], self.frecv.at[way], self.row(1 - 2 * way))

    def across(self, d, r):
        where = self.whole.at[self.row(d), r]
        source = self.own.at[r] if d == 0 else where
        return self.copy(source, where, self.ssend.at[d, r], self.srecv.at[d, r], self.prow + 1 - 2 * self.core)

    def start(self):
        for r in range(2):
            for way in range(2):
                self.near(way, (r + way) % 2).start()
        for r in range(2):
            self.across(0, r).start()

    def forward(self):
        for way in range(2):
            self.near(way, way).wait_recv()
            self.far(way).start()
            self.across(3 - 2 * way, way).start()

    def pass_on(self):
        for way in range(2):
            self.near(way, 1 - way).wait_recv()
            self.across(3 - 2 * way, 1 - way).start()

    def last(self):
        for way in range(2):
            self.far(way).wait_recv()
            self.across(2, way).start()

    def finish(self):
        for d in range(4):
            for r in range(2):
                self.across(d, r).wait()
        for way in range(2):
            self.far(way).wait_send()
            for r in range(2):
                self.near(way, r).wait_send()


def factor_kernel(
    first_ref, target_ref, diag_ref, top_ref, panel_ref,
    hi_ref, lo_ref, tf_ref, pf_ref, inc_ref, marks_ref,
    w, m, t, left, right, tops, masked, mark, first, target, local, *sems,
):
    grid_rows, blocks, rows, n = inc_ref.shape
    diag = Ring(diag_ref, w, sems[0:6], True)
    top = Ring(top_ref, tops, sems[6:12], False)
    panels = Panels(panel_ref, inc_ref, sems[12:18])
    msend, mrecv = sems[18:]
    prow, pcol = diag.prow, lax.axis_index("pcol")
    own_rows = pl.ds(pl.multiple_of(pcol * diag.rows, diag.rows), diag.rows)

    barrier = pltpu.get_barrier_semaphore()
    peers = [diag.at(diag.x + d, diag.z) for d in range(1, NX)]
    peers += [diag.at(diag.x, diag.z + 1), diag.at(diag.x, diag.z - 1)]
    peers += [(lax.rem(prow + d, grid_rows), pcol) for d in range(1, grid_rows)]
    for peer in peers:
        pl.semaphore_signal(barrier, inc=1, device_id=peer, device_id_type=MESH)
    keep_diag = pltpu.make_async_copy(diag_ref, w.at[own_rows], local.at[0])
    keep_diag.start()
    keep_top = pltpu.make_async_copy(top_ref, tops.at[own_rows], local.at[1])
    keep_top.start()
    keep_panel = pltpu.make_async_copy(panel_ref, inc_ref.at[prow], local.at[2])
    keep_panel.start()
    take_first = pltpu.make_async_copy(first_ref, first, local.at[4])
    take_first.start()
    take_target = pltpu.make_async_copy(target_ref, target, local.at[5])
    take_target.start()
    take_first.wait()
    take_target.wait()
    lane = lax.broadcasted_iota(jnp.int32, mark.shape, 1)
    word = jnp.where(lane == 0, target[0], target[1])
    for r in range(blocks):
        word = jnp.where(lane == blocks + r, first[r], word)
    mark[...] = word
    pl.semaphore_wait(barrier, len(peers))

    diag.start()

    def mcopy(d):
        return pltpu.make_async_remote_copy(
            mark, marks_ref.at[prow], msend.at[d - 1], mrecv.at[d - 1],
            device_id=(lax.rem(prow + d, grid_rows), pcol), device_id_type=MESH,
        )

    for d in range(1, grid_rows):
        mcopy(d).start()
    keep_mark = pltpu.make_async_copy(mark, marks_ref.at[prow], local.at[3])
    keep_mark.start()
    panels.start()
    keep_panel.wait()
    for r in range(blocks):
        for j in range(n // rows):
            cut = slice(j * rows, j * rows + rows)
            piece = inc_ref[prow, r, :, cut]
            masked[r * rows:(r + 1) * rows, cut] = jnp.where(first[r] <= j, piece, jnp.zeros_like(piece))

    keep_diag.wait()
    keep_top.wait()
    every = range(NX)
    diag.across(every)
    top.start()
    for hop in range(NZ // 2):
        diag.hop(hop, every)
    top.across(every)
    panels.forward()
    diag.finish(every)
    diag.drain(every)

    def before(b):
        if b == 1:
            panels.pass_on()
        if b == 5:
            panels.last()
        if b == 6:
            top.finish(every)

    def tick(b, s):
        hop = {(1, 0): 0, (2, 1): 1, (3, 2): 2, (4, 3): 3}.get((b, s))
        if hop is not None:
            top.hop(hop, every)

    def solve(x, out, j, piece):
        at = slice(512 * piece, 512 * piece + 512)
        out[at, 256 * j:256 * j + 256] = solve_part(x[at, :], hi_ref, lo_ref, j)

    def extra(b):
        own = {3: [0], 5: [1], 7: [2]}.get(b, [])
        tall = {6: [0, 1], 7: [2]}.get(b, [])
        work = [functools.partial(solve, masked, pf_ref, j, 0) for j in own]
        return work + [functools.partial(solve, tops, tf_ref, j, piece) for j in tall for piece in range(n // 512)]

    eliminate(w, m, t, left, right, hi_ref, lo_ref, 32, 12, before, tick, extra)
    solve(masked, pf_ref, 3, 0)
    for piece in range(n // 512):
        solve(tops, tf_ref, 3, piece)
    panels.finish()
    keep_mark.wait()
    top.drain(every)
    for d in range(1, grid_rows):
        mcopy(d).wait()


def factor(first_block, target, diag_one, top_rows, panel_one, grid_rows):
    n = diag_one.shape[1]
    blocks = first_block.shape[0]
    rows = panel_one.shape[0] // blocks
    vmem = pl.BlockSpec(memory_space=pltpu.VMEM)
    hbm = pl.BlockSpec(memory_space=pltpu.HBM)
    dma = pltpu.SemaphoreType.DMA
    ring = [dma((NX - 1,)), dma((NX,))] + [dma((NX, 2, NZ // 2))] * 2 + [dma((NX, NZ))] * 2
    here = lambda v: pltpu.with_memory_space_constraint(v, pltpu.HBM)
    return pl.pallas_call(
        factor_kernel,
        out_shape=[
            jax.ShapeDtypeStruct((n, n), BF16),
            jax.ShapeDtypeStruct((n, n), BF16),
            jax.ShapeDtypeStruct((n, n), BF16),
            jax.ShapeDtypeStruct(panel_one.shape, BF16),
            jax.ShapeDtypeStruct((grid_rows, blocks, rows, n), BF16),
            jax.ShapeDtypeStruct((grid_rows, 8, 128), jnp.int32),
        ],
        in_specs=[hbm] * 5,
        out_specs=[vmem] * 6,
        scratch_shapes=[
            pltpu.VMEM((n, n), F32),
            pltpu.VMEM((NB, NB), F32),
            pltpu.VMEM((NB, NB), F32),
            pltpu.VMEM((2 * 3 * NB, n), BF16),
            pltpu.VMEM((2 * 3 * NB, n), BF16),
            pltpu.VMEM((n, n), BF16),
            pltpu.VMEM(panel_one.shape, BF16),
            pltpu.VMEM((8, 128), jnp.int32),
            pltpu.SMEM(first_block.shape, jnp.int32),
            pltpu.SMEM(target.shape, jnp.int32),
            dma((6,)),
        ] + ring + ring
        + [dma((2, 2))] * 2 + [dma((2,))] * 2 + [dma((4, 2))] * 2 + [dma((grid_rows - 1,))] * 2,
        compiler_params=pltpu.CompilerParams(
            collective_id=0, has_side_effects=True, vmem_limit_bytes=28 << 20
        ),
    )(here(first_block), here(target), here(diag_one), here(top_rows), here(panel_one.reshape(blocks, rows, n)))


QUAD = 4


def apply_kernel(
    marks, hi_ref, lo_ref, tf_ref, pf_ref, inc_ref, two_ref, diag_ref,
    pf_out, tf_out, dn_out, pn_out, two, diag, acc, x, solved, sems,
):
    sources, blocks, rows, n = inc_ref.shape
    local = diag.shape[0]
    prow, pcol = lax.axis_index("prow"), lax.axis_index("pcol")
    own = pl.ds(pl.multiple_of(pcol * local, local), local)
    load_two = pltpu.make_async_copy(two_ref, two, sems.at[0])
    load_two.start()
    load_diag = pltpu.make_async_copy(diag_ref, diag, sems.at[1])
    load_diag.start()
    save_pf = pltpu.make_async_copy(pf_ref, pf_out, sems.at[2])
    save_pf.start()
    save_tf = pltpu.make_async_copy(tf_ref.at[own], tf_out, sems.at[3])
    save_tf.start()
    load_diag.wait()
    diag[...] = diag[...] - ndot(tf_ref[own, :], tf_ref[...])
    save_dn = pltpu.make_async_copy(diag, dn_out, sems.at[4])
    save_dn.start()
    load_two.wait()
    acc[...] = two[...].astype(F32)

    def quad(q, carry):
        slots, some, firsts, picks = [], [], [], []
        for i in range(QUAD):
            p = q * QUAD + i
            slot, which, here = 0, 0, False
            for r in range(blocks):
                to = marks[p, 0, r]
                mine = to // (blocks * lax.axis_size("pcol")) == prow
                slot = jnp.where(mine, lax.rem(to, blocks), slot)
                which = jnp.where(mine, r, which)
                here = mine | here
            slots.append(slot)
            some.append(here)
            first = jnp.where(here, marks[p, 0, blocks + which], n)
            firsts.append(first)
            picks.append(which)
        anyone = some[0]
        for here in some[1:]:
            anyone = anyone | here

        @pl.when(anyone)
        def _():
            for i in range(QUAD):
                for j in range(n // rows):
                    cut = slice(j * rows, j * rows + rows)
                    piece = inc_ref[q * QUAD + i, picks[i], :, cut]
                    x[i * rows:(i + 1) * rows, cut] = jnp.where(firsts[i] <= j, piece, jnp.zeros_like(piece))
            for j in range(n // 256):
                solved[:, 256 * j:256 * j + 256] = solve_part(x, hi_ref, lo_ref, j)
            for j in range(n // 256):
                cut = slice(256 * j, 256 * j + 256)
                update = ndot(solved[...], tf_ref[cut, :]).astype(BF16).astype(F32)
                for i in range(QUAD):
                    at = pl.ds(pl.multiple_of(slots[i] * rows, rows), rows)
                    acc[at, cut] = acc[at, cut] - update[i * rows:(i + 1) * rows, :]

        return carry

    lax.fori_loop(0, sources // QUAD, quad, 0)
    save_pn = pltpu.make_async_copy(acc, pn_out, sems.at[5])
    save_pn.start()
    for save in (save_pf, save_tf, save_dn, save_pn):
        save.wait()


def apply(marks, hi, lo, tf, pf, incoming, two, diag_two):
    n = hi.shape[0]
    rows = incoming.shape[2]
    local = diag_two.shape[0]
    smem = pl.BlockSpec(memory_space=pltpu.SMEM)
    vmem = pl.BlockSpec(memory_space=pltpu.VMEM)
    hbm = pl.BlockSpec(memory_space=pltpu.HBM)
    here = lambda v: pltpu.with_memory_space_constraint(v, pltpu.HBM)
    return pl.pallas_call(
        apply_kernel,
        out_shape=[
            jax.ShapeDtypeStruct(pf.shape, BF16),
            jax.ShapeDtypeStruct((local, n), BF16),
            jax.ShapeDtypeStruct((local, n), F32),
            jax.ShapeDtypeStruct(two.shape, F32),
        ],
        in_specs=[smem, vmem, vmem, vmem, vmem, vmem, hbm, hbm],
        out_specs=[hbm] * 4,
        scratch_shapes=[
            pltpu.VMEM(two.shape, BF16),
            pltpu.VMEM((local, n), F32),
            pltpu.VMEM(two.shape, F32),
            pltpu.VMEM((QUAD * rows, n), BF16),
            pltpu.VMEM((QUAD * rows, n), BF16),
            pltpu.SemaphoreType.DMA((6,)),
        ],
        compiler_params=pltpu.CompilerParams(vmem_limit_bytes=20 << 20),
    )(marks, hi, lo, tf, pf, incoming, here(two), here(diag_two))


def on_device(diag_one, top_rows, panel_one, first_block, target, diag_two, panel_two):
    hi, lo, tf, pf, incoming, marks = factor(
        first_block, target, diag_one, top_rows, panel_one, lax.axis_size("prow")
    )
    return tuple(apply(marks, hi, lo, tf, pf, incoming, panel_two, diag_two))


def solution(mesh):
    whole = P(("prow", "pcol"), None)
    blocks = P(("prow", "pcol"))
    part = P("pcol", None)
    return jax.shard_map(
        on_device,
        mesh=mesh,
        in_specs=(part, part, whole, blocks, blocks, part, whole),
        out_specs=(whole, part, part, whole),
        check_vma=False,
    )
```

```python
import functools

import jax
import jax.numpy as jnp
from jax import lax
from jax.experimental import pallas as pl
from jax.experimental.pallas import tpu as pltpu
from jax.sharding import PartitionSpec as P

F32, BF16 = jnp.float32, jnp.bfloat16
NB = 128


def split2(x):
    hi = x.astype(BF16)
    lo = (x - hi.astype(F32)).astype(BF16)
    return hi, lo


def tdot(left, right):
    return lax.dot_general(left, right, (((0,), (0,)), ((), ())), preferred_element_type=F32)


def row_bcast(x, k):
    return jnp.broadcast_to(x[k:k + 1, :], (8, x.shape[1]))


def factor_block(m_ref, t_ref, G, p, work, tick):
    n = NB
    sub = lax.broadcasted_iota(jnp.int32, (8, n), 0)
    lane = lax.broadcasted_iota(jnp.int32, (8, n), 1)
    groups = n // G
    nch = G // 8
    done = 0
    for s in range(groups):
        r0 = s * G
        tick(s)
        band = [m_ref[r0 + 8 * c:r0 + 8 * c + 8, :] for c in range(nch)]
        window = {}
        dvec = [None] * nch

        def spread(j):
            for c in range(j // 8, nch):
                window[j, c] = jnp.broadcast_to(band[c][:, r0 + j:r0 + j + 1], (8, n))

        for j in range(min(p, G)):
            spread(j)
        for k in range(G):
            until = len(work) * (s * G + k + 1) // n
            while done < until:
                work[done]()
                done += 1
            kc, kr = k // 8, k % 8
            piv = row_bcast(window[k, kc], kr)
            dvec[kc] = piv if kr == 0 else jnp.where(sub >= kr, piv, dvec[kc])
            rd = 1.0 / piv
            mult = {c: window[k, c] * rd for c in range(kc, nch)}
            mult[kc] = jnp.where(sub > kr, mult[kc], 0.0)
            for j in range(k + 1, min(k + p, G)):
                jc = j // 8
                other = row_bcast(window[k, jc], j % 8)
                for c in range(jc, nch):
                    window[j, c] = window[j, c] - mult[c] * other
            here = lane == r0 + k
            row = jnp.where(here, 1.0, row_bcast(band[kc], kr))
            for c in range(kc, nch):
                if c == kc:
                    old = jnp.where(here & (sub >= kr), (sub == kr).astype(F32), band[c])
                else:
                    old = jnp.where(here, 0.0, band[c])
                band[c] = old - mult[c] * row
            if k + p < G:
                spread(k + p)
            for c in range(kc, nch):
                del window[k, c]
        for c in range(nch):
            band[c] = band[c] * lax.rsqrt(dvec[c])
            upper = lane > sub + (r0 + 8 * c)
            t_ref[r0 + 8 * c:r0 + 8 * c + 8, :] = jnp.where(upper, 0.0, band[c])
            band[c] = jnp.where(upper & (lane < r0 + G), 0.0, band[c])
        if r0 + G < n:
            r = jnp.concatenate(band, axis=0)
            hi, lo = split2(r)
            prod = tdot(jnp.concatenate([hi, hi, lo], axis=0), jnp.concatenate([hi, lo, hi], axis=0))
            lane_all = lax.broadcasted_iota(jnp.int32, (n - r0 - G, n), 1)
            keep = (lane_all < r0) | (lane_all >= r0 + G)
            m_ref[r0 + G:, :] = jnp.where(keep, m_ref[r0 + G:, :], 0.0) - prod[r0 + G:, :]
    while done < len(work):
        work[done]()
        done += 1


def blk(i, j=None):
    return slice(NB * i, NB * (i + 1 if j is None else j))


def eliminate(w, m, t, left, right, hi_ref, lo_ref, G, p, before, tick, extra):
    n = w.shape[1]
    steps = n // NB
    slots = left.shape[0] // (3 * NB)

    def update(i, k0, k1, start, stop, fresh):
        at = 3 * NB * (k0 % slots)
        span = slice(at, at + 3 * NB * (k1 - k0))
        prod = tdot(left[span, blk(i)], right[span, blk(start, stop)])
        if fresh:
            w[blk(i), blk(start, stop)] = -prod
        else:
            w[blk(i), blk(start, stop)] = w[blk(i), blk(start, stop)] - prod

    for b in range(steps):
        before(b)
        if b > 0:
            update(b, b - 1, b, b, b + 1, False)
        m[...] = w[blk(b), blk(b)]
        work = []
        for i in range(b, steps):
            if b == 0:
                continue
            k0 = b - 1
            if k0 > 0:
                work.append(functools.partial(update, i, k0, b, 0, k0, False))
            for c in range(k0, b):
                work.append(functools.partial(update, i, c, b, c, c + 1, True))
            first = max(i, b + 1)
            if first < steps:
                work.append(functools.partial(update, i, k0, b, first, steps, False))
        work += extra(b)
        factor_block(m, t, G, p, work, functools.partial(tick, b))
        th, tl = split2(t[...])
        tt = jnp.concatenate([th, th, tl], axis=1)
        at = 3 * NB * (b % slots)
        one, two, three = (slice(at + NB * q, at + NB * q + NB) for q in range(3))
        for start, stop in ((0, b), (b, b + 1), (b + 1, steps)):
            if start == stop:
                continue
            cut = blk(start, stop)
            if start == b:
                rh, rl = th, tl
            else:
                wh, wl = split2(w[blk(b), cut])
                r = jnp.dot(tt, jnp.concatenate([wh, wl, wh], axis=0), preferred_element_type=F32)
                rh, rl = split2(r)
            if start > b:
                left[one, cut] = rh
                left[two, cut] = rh
                left[three, cut] = rl
            else:
                hi_ref[blk(b), cut] = rh
                lo_ref[blk(b), cut] = rl
            right[one, cut] = rh
            right[two, cut] = rl
            right[three, cut] = rh
        if b + 1 < steps:
            hi_ref[blk(b), blk(b + 1, steps)] = jnp.zeros((NB, n - NB * (b + 1)), BF16)
            lo_ref[blk(b), blk(b + 1, steps)] = jnp.zeros((NB, n - NB * (b + 1)), BF16)


NX, NZ = 4, 8
MESH = pl.DeviceIdType.MESH


def ndot(left, right):
    return lax.dot_general(left, right, (((1,), (1,)), ((), ())), preferred_element_type=F32)


def solve_part(rows, hi_ref, lo_ref, j):
    cut, upto = slice(256 * j, 256 * j + 256), slice(0, 256 * j + 256)
    return (ndot(rows[:, upto], hi_ref[cut, upto]) + ndot(rows[:, upto], lo_ref[cut, upto])).astype(BF16)


class Ring:
    def __init__(self, own, whole, sems, trim):
        self.own, self.whole, self.trim = own, whole, trim
        self.xsend, self.xrecv, self.zsend, self.zrecv, self.ssend, self.srecv = sems
        self.rows, self.n = own.shape
        self.prow, pcol = lax.axis_index("prow"), lax.axis_index("pcol")
        self.core = lax.rem(self.prow, 2)
        self.x, self.z = pcol // NZ, lax.rem(pcol, NZ)
        self.sibling = (self.prow + 1 - 2 * self.core, pcol)
        self.hops = (NZ // 2, NZ // 2 - 1)

    def at(self, x, z):
        return (self.prow, lax.rem(x + NX, NX) * NZ + lax.rem(z + NZ, NZ))

    def place(self, xs, zz):
        skip = self.n // NX * xs if self.trim else 0
        width = (self.n - skip) // 2
        row = pl.multiple_of((xs * NZ + zz) * self.rows, self.rows)
        return pl.ds(row, self.rows), pl.ds(pl.multiple_of(skip + self.core * width, 128), width)

    def xcopy(self, xs, d):
        where = self.place(xs, self.z)
        return pltpu.make_async_remote_copy(
            self.own.at[:, where[1]], self.whole.at[where], self.xsend.at[d - 1], self.xrecv.at[xs],
            device_id=self.at(xs + d, self.z), device_id_type=MESH,
        )

    def scopy(self, xs, zz, slot):
        where = self.whole.at[self.place(xs, zz)]
        return pltpu.make_async_remote_copy(
            where, where, self.ssend.at[xs, slot], self.srecv.at[xs, slot],
            device_id=self.sibling, device_id_type=MESH,
        )

    def zcopy(self, xs, zz, way, hop):
        where = self.whole.at[self.place(xs, zz)]
        return pltpu.make_async_remote_copy(
            where, where, self.zsend.at[xs, way, hop], self.zrecv.at[xs, way, hop],
            device_id=self.at(self.x, self.z + 1 - 2 * way), device_id_type=MESH,
        )

    def start(self):
        for xs in range(NX):
            @pl.when(self.x == xs)
            def _():
                for d in range(1, NX):
                    self.xcopy(xs, d).start()

    def across(self, groups):
        for xs in groups:
            @pl.when(self.x != xs)
            def _():
                self.xcopy(xs, 1).wait_recv()
            for way in range(2):
                self.zcopy(xs, self.z, way, 0).start()
        for xs in groups:
            @pl.when(self.x != xs)
            def _():
                self.scopy(xs, self.z, 0).start()

    def hop(self, hop, groups):
        for xs in groups:
            for way in range(2):
                if hop >= self.hops[way]:
                    continue
                back = self.z - hop - 1 if way == 0 else self.z + hop + 1
                back = lax.rem(back + NZ, NZ)
                self.zcopy(xs, back, way, hop).wait_recv()
                if hop + 1 < self.hops[way]:
                    self.zcopy(xs, back, way, hop + 1).start()
                self.scopy(xs, back, 1 + hop + way * (NZ // 2)).start()

    def finish(self, groups):
        for xs in groups:
            @pl.when(self.x != xs)
            def _():
                self.scopy(xs, self.z, 0).wait_recv()
            for slot in range(1, NZ):
                self.scopy(xs, self.z, slot).wait_recv()

    def drain(self, groups):
        for xs in groups:
            @pl.when(self.x == xs)
            def _():
                for d in range(1, NX):
                    self.xcopy(xs, d).wait_send()

            @pl.when(self.x != xs)
            def _():
                self.scopy(xs, self.z, 0).wait_send()
            for way in range(2):
                for hop in range(self.hops[way]):
                    self.zcopy(xs, self.z, way, hop).wait_send()
            for slot in range(1, NZ):
                self.scopy(xs, self.z, slot).wait_send()


class Panels:
    def __init__(self, own, whole, sems):
        self.own, self.whole = own, whole
        self.ysend, self.yrecv, self.fsend, self.frecv, self.ssend, self.srecv = sems
        self.prow, self.pcol = lax.axis_index("prow"), lax.axis_index("pcol")
        self.grid_rows = lax.axis_size("prow")
        self.core = lax.rem(self.prow, 2)

    def row(self, d):
        return lax.rem(self.prow + 2 * d + self.grid_rows, self.grid_rows)

    def copy(self, source, target, send, recv, row):
        return pltpu.make_async_remote_copy(
            source, target, send, recv, device_id=(row, self.pcol), device_id_type=MESH
        )

    def near(self, way, r):
        return self.copy(
            self.own.at[r], self.whole.at[self.prow, r], self.ysend.at[way, r], self.yrecv.at[way, r],
            self.row(1 - 2 * way),
        )

    def far(self, way):
        where = self.whole.at[self.row(2 * way - 1), way]
        return self.copy(where, where, self.fsend.at[way], self.frecv.at[way], self.row(1 - 2 * way))

    def across(self, d, r):
        where = self.whole.at[self.row(d), r]
        source = self.own.at[r] if d == 0 else where
        return self.copy(source, where, self.ssend.at[d, r], self.srecv.at[d, r], self.prow + 1 - 2 * self.core)

    def start(self):
        for r in range(2):
            for way in range(2):
                self.near(way, (r + way) % 2).start()
        for r in range(2):
            self.across(0, r).start()

    def forward(self):
        for way in range(2):
            self.near(way, way).wait_recv()
            self.far(way).start()
            self.across(3 - 2 * way, way).start()

    def pass_on(self):
        for way in range(2):
            self.near(way, 1 - way).wait_recv()
            self.across(3 - 2 * way, 1 - way).start()

    def last(self):
        for way in range(2):
            self.far(way).wait_recv()
            self.across(2, way).start()

    def finish(self):
        for d in range(4):
            for r in range(2):
                self.across(d, r).wait()
        for way in range(2):
            self.far(way).wait_send()
            for r in range(2):
                self.near(way, r).wait_send()


def factor_kernel(
    first_ref, target_ref, diag_ref, top_ref, panel_ref,
    hi_ref, lo_ref, tf_ref, pf_ref, inc_ref, marks_ref,
    w, m, t, left, right, tops, masked, mark, first, target, local, *sems,
):
    grid_rows, blocks, rows, n = inc_ref.shape
    diag = Ring(diag_ref, w, sems[0:6], True)
    top = Ring(top_ref, tops, sems[6:12], False)
    panels = Panels(panel_ref, inc_ref, sems[12:18])
    msend, mrecv = sems[18:]
    prow, pcol = diag.prow, lax.axis_index("pcol")
    own_rows = pl.ds(pl.multiple_of(pcol * diag.rows, diag.rows), diag.rows)

    barrier = pltpu.get_barrier_semaphore()
    peers = [diag.at(diag.x + d, diag.z) for d in range(1, NX)]
    peers += [diag.at(diag.x, diag.z + 1), diag.at(diag.x, diag.z - 1)]
    peers += [(lax.rem(prow + d, grid_rows), pcol) for d in range(1, grid_rows)]
    for peer in peers:
        pl.semaphore_signal(barrier, inc=1, device_id=peer, device_id_type=MESH)
    keep_diag = pltpu.make_async_copy(diag_ref, w.at[own_rows], local.at[0])
    keep_diag.start()
    keep_top = pltpu.make_async_copy(top_ref, tops.at[own_rows], local.at[1])
    keep_top.start()
    keep_panel = pltpu.make_async_copy(panel_ref, inc_ref.at[prow], local.at[2])
    keep_panel.start()
    take_first = pltpu.make_async_copy(first_ref, first, local.at[4])
    take_first.start()
    take_target = pltpu.make_async_copy(target_ref, target, local.at[5])
    take_target.start()
    take_first.wait()
    take_target.wait()
    lane = lax.broadcasted_iota(jnp.int32, mark.shape, 1)
    word = jnp.where(lane == 0, target[0], target[1])
    for r in range(blocks):
        word = jnp.where(lane == blocks + r, first[r], word)
    mark[...] = word
    pl.semaphore_wait(barrier, len(peers))

    diag.start()

    def mcopy(d):
        return pltpu.make_async_remote_copy(
            mark, marks_ref.at[prow], msend.at[d - 1], mrecv.at[d - 1],
            device_id=(lax.rem(prow + d, grid_rows), pcol), device_id_type=MESH,
        )

    for d in range(1, grid_rows):
        mcopy(d).start()
    keep_mark = pltpu.make_async_copy(mark, marks_ref.at[prow], local.at[3])
    keep_mark.start()
    panels.start()
    keep_panel.wait()
    for r in range(blocks):
        for j in range(n // rows):
            cut = slice(j * rows, j * rows + rows)
            piece = inc_ref[prow, r, :, cut]
            masked[r * rows:(r + 1) * rows, cut] = jnp.where(first[r] <= j, piece, jnp.zeros_like(piece))

    keep_diag.wait()
    keep_top.wait()
    every = range(NX)
    diag.across(every)
    top.start()
    for hop in range(NZ // 2):
        diag.hop(hop, every)
    top.across(every)
    panels.forward()
    diag.finish(every)
    diag.drain(every)

    def before(b):
        if b == 1:
            panels.pass_on()
        if b == 5:
            panels.last()
        if b == 6:
            top.finish(every)

    def tick(b, s):
        hop = {(1, 0): 0, (2, 1): 1, (3, 2): 2, (4, 3): 3}.get((b, s))
        if hop is not None:
            top.hop(hop, every)

    def solve(x, out, j, piece):
        at = slice(512 * piece, 512 * piece + 512)
        out[at, 256 * j:256 * j + 256] = solve_part(x[at, :], hi_ref, lo_ref, j)

    def extra(b):
        own = {3: [0], 5: [1], 7: [2]}.get(b, [])
        tall = {6: [0, 1], 7: [2]}.get(b, [])
        work = [functools.partial(solve, masked, pf_ref, j, 0) for j in own]
        return work + [functools.partial(solve, tops, tf_ref, j, piece) for j in tall for piece in range(n // 512)]

    eliminate(w, m, t, left, right, hi_ref, lo_ref, 32, 12, before, tick, extra)
    solve(masked, pf_ref, 3, 0)
    for piece in range(n // 512):
        solve(tops, tf_ref, 3, piece)
    panels.finish()
    keep_mark.wait()
    top.drain(every)
    for d in range(1, grid_rows):
        mcopy(d).wait()


def factor(first_block, target, diag_one, top_rows, panel_one, grid_rows):
    n = diag_one.shape[1]
    blocks = first_block.shape[0]
    rows = panel_one.shape[0] // blocks
    vmem = pl.BlockSpec(memory_space=pltpu.VMEM)
    hbm = pl.BlockSpec(memory_space=pltpu.HBM)
    dma = pltpu.SemaphoreType.DMA
    ring = [dma((NX - 1,)), dma((NX,))] + [dma((NX, 2, NZ // 2))] * 2 + [dma((NX, NZ))] * 2
    here = lambda v: pltpu.with_memory_space_constraint(v, pltpu.HBM)
    return pl.pallas_call(
        factor_kernel,
        out_shape=[
            jax.ShapeDtypeStruct((n, n), BF16),
            jax.ShapeDtypeStruct((n, n), BF16),
            jax.ShapeDtypeStruct((n, n), BF16),
            jax.ShapeDtypeStruct(panel_one.shape, BF16),
            jax.ShapeDtypeStruct((grid_rows, blocks, rows, n), BF16),
            jax.ShapeDtypeStruct((grid_rows, 8, 128), jnp.int32),
        ],
        in_specs=[hbm] * 5,
        out_specs=[vmem] * 6,
        scratch_shapes=[
            pltpu.VMEM((n, n), F32),
            pltpu.VMEM((NB, NB), F32),
            pltpu.VMEM((NB, NB), F32),
            pltpu.VMEM((2 * 3 * NB, n), BF16),
            pltpu.VMEM((2 * 3 * NB, n), BF16),
            pltpu.VMEM((n, n), BF16),
            pltpu.VMEM(panel_one.shape, BF16),
            pltpu.VMEM((8, 128), jnp.int32),
            pltpu.SMEM(first_block.shape, jnp.int32),
            pltpu.SMEM(target.shape, jnp.int32),
            dma((6,)),
        ] + ring + ring
        + [dma((2, 2))] * 2 + [dma((2,))] * 2 + [dma((4, 2))] * 2 + [dma((grid_rows - 1,))] * 2,
        compiler_params=pltpu.CompilerParams(
            collective_id=0, has_side_effects=True, vmem_limit_bytes=28 << 20
        ),
    )(here(first_block), here(target), here(diag_one), here(top_rows), here(panel_one.reshape(blocks, rows, n)))


QUAD = 4


def apply_kernel(
    marks, hi_ref, lo_ref, tf_ref, pf_ref, inc_ref, two_ref, diag_ref,
    pf_out, tf_out, dn_out, pn_out, two, diag, acc, x, solved, sems,
):
    sources, blocks, rows, n = inc_ref.shape
    local = diag.shape[0]
    prow, pcol = lax.axis_index("prow"), lax.axis_index("pcol")
    own = pl.ds(pl.multiple_of(pcol * local, local), local)
    load_two = pltpu.make_async_copy(two_ref, two, sems.at[0])
    load_two.start()
    load_diag = pltpu.make_async_copy(diag_ref, diag, sems.at[1])
    load_diag.start()
    save_pf = pltpu.make_async_copy(pf_ref, pf_out, sems.at[2])
    save_pf.start()
    save_tf = pltpu.make_async_copy(tf_ref.at[own], tf_out, sems.at[3])
    save_tf.start()

    def place(p):
        slot, which, first = 0, 0, n
        for r in range(blocks):
            to = marks[p, 0, r]
            mine = to // (blocks * lax.axis_size("pcol")) == prow
            slot = jnp.where(mine, lax.rem(to, blocks), slot)
            which = jnp.where(mine, r, which)
            first = jnp.where(mine, marks[p, 0, blocks + r], first)
        return slot, which, first

    def solve(q, slots):
        for i in range(QUAD):
            slot, which, first = place(q * QUAD + i)
            slots.append(slot)
            for j in range(n // rows):
                cut = slice(j * rows, j * rows + rows)
                piece = inc_ref[q * QUAD + i, which, :, cut]
                x[q, i * rows:(i + 1) * rows, cut] = jnp.where(first <= j, piece, jnp.zeros_like(piece))
        for j in range(n // 256):
            solved[q, :, 256 * j:256 * j + 256] = solve_part(x.at[q], hi_ref, lo_ref, j)

    def update(q, slots):
        for j in range(n // 256):
            cut = slice(256 * j, 256 * j + 256)
            change = ndot(solved[q], tf_ref[cut, :]).astype(BF16).astype(F32)
            for i in range(QUAD):
                at = pl.ds(pl.multiple_of(slots[i] * rows, rows), rows)
                acc[at, cut] = acc[at, cut] - change[i * rows:(i + 1) * rows, :]

    slots = [[] for _ in range(sources // QUAD)]
    solve(0, slots[0])
    load_two.wait()
    acc[...] = two[...].astype(F32)
    load_diag.wait()
    diag[...] = diag[...] - ndot(tf_ref[own, :], tf_ref[...])
    save_dn = pltpu.make_async_copy(diag, dn_out, sems.at[4])
    save_dn.start()
    update(0, slots[0])
    for q in range(1, sources // QUAD):
        solve(q, slots[q])
        update(q, slots[q])
    save_pn = pltpu.make_async_copy(acc, pn_out, sems.at[5])
    save_pn.start()
    for save in (save_pf, save_tf, save_dn, save_pn):
        save.wait()


def apply(marks, hi, lo, tf, pf, incoming, two, diag_two):
    n = hi.shape[0]
    rows = incoming.shape[2]
    local = diag_two.shape[0]
    smem = pl.BlockSpec(memory_space=pltpu.SMEM)
    vmem = pl.BlockSpec(memory_space=pltpu.VMEM)
    hbm = pl.BlockSpec(memory_space=pltpu.HBM)
    here = lambda v: pltpu.with_memory_space_constraint(v, pltpu.HBM)
    return pl.pallas_call(
        apply_kernel,
        out_shape=[
            jax.ShapeDtypeStruct(pf.shape, BF16),
            jax.ShapeDtypeStruct((local, n), BF16),
            jax.ShapeDtypeStruct((local, n), F32),
            jax.ShapeDtypeStruct(two.shape, F32),
        ],
        in_specs=[smem, vmem, vmem, vmem, vmem, vmem, hbm, hbm],
        out_specs=[hbm] * 4,
        scratch_shapes=[
            pltpu.VMEM(two.shape, BF16),
            pltpu.VMEM((local, n), F32),
            pltpu.VMEM(two.shape, F32),
            pltpu.VMEM((incoming.shape[0] // QUAD, QUAD * rows, n), BF16),
            pltpu.VMEM((incoming.shape[0] // QUAD, QUAD * rows, n), BF16),
            pltpu.SemaphoreType.DMA((6,)),
        ],
        compiler_params=pltpu.CompilerParams(vmem_limit_bytes=20 << 20),
    )(marks, hi, lo, tf, pf, incoming, here(two), here(diag_two))


def on_device(diag_one, top_rows, panel_one, first_block, target, diag_two, panel_two):
    hi, lo, tf, pf, incoming, marks = factor(
        first_block, target, diag_one, top_rows, panel_one, lax.axis_size("prow")
    )
    return tuple(apply(marks, hi, lo, tf, pf, incoming, panel_two, diag_two))


def solution(mesh):
    whole = P(("prow", "pcol"), None)
    blocks = P(("prow", "pcol"))
    part = P("pcol", None)
    return jax.shard_map(
        on_device,
        mesh=mesh,
        in_specs=(part, part, whole, blocks, blocks, part, whole),
        out_specs=(whole, part, part, whole),
        check_vma=False,
    )
```
